32 devices in a mesh: dp: 8 (over y, x, core), tensor: 4 (over z).
Axes of the slice: x: 2, y: 2, z: 4, core: 2. Of those that a mesh axis runs over, the one named last changes fastest.
Arguments:
- tokens: bfloat16 [16384, 768], P('dp'), may hold values from -24 to 24
- lengths: int32 [8, 8], P('dp'), may hold values from 1 to 512, 2048 in all within a row
- w_qkv: bfloat16 [3, 768, 768], P(None, None, 'tensor'), may hold values from -0.21875 to 0.21875
- b_qv: bfloat16 [2, 768], P(None, 'tensor'), may hold values from -3 to 3
- w_out: bfloat16 [768, 768], P('tensor'), may hold values from -0.875 to 0.875
- b_out: bfloat16 [768], replicated, may hold values from -3 to 3
- ln1_gain: bfloat16 [768], replicated, may hold values from 0.099609375 to 1.8984375
- ln1_bias: bfloat16 [768], replicated, may hold values from -3 to 3
- w_up: bfloat16 [768, 3072], P(None, 'tensor'), may hold values from -0.21875 to 0.21875
- b_up: bfloat16 [3072], P('tensor'), may hold values from -3 to 3
- w_down: bfloat16 [3072, 768], P('tensor'), may hold values from -0.109375 to 0.109375
- b_down: bfloat16 [768], replicated, may hold values from -3 to 3
- ln2_gain: bfloat16 [768], replicated, may hold values from 0.099609375 to 1.8984375
- ln2_bias: bfloat16 [768], replicated, may hold values from -3 to 3
- cotangent: bfloat16 [16384, 768], P('dp'), may hold values from -24 to 24
Outputs:
- layer_out: bfloat16 [16384, 768], P(('dp', 'tensor'))
- input_grad: bfloat16 [16384, 768], P(('dp', 'tensor'))
- grad_qkv: float32 [3, 768, 768], P(None, 'dp', 'tensor')
- grad_qv_bias: float32 [2, 768], P(None, 'tensor')
- grad_out: float32 [768, 768], P('tensor', 'dp')
- grad_out_bias: float32 [768], P('dp')
- grad_norm1_gain: float32 [768], P('dp')
- grad_norm1_bias: float32 [768], P('dp')
- grad_up: float32 [768, 3072], P('dp', 'tensor')
- grad_up_bias: float32 [3072], P('tensor')
- grad_down: float32 [3072, 768], P('tensor', 'dp')
- grad_down_bias: float32 [768], P('dp')
- grad_norm2_gain: float32 [768], P('dp')
- grad_norm2_bias: float32 [768], P('dp')
The draws below stay inside these ranges and needn't reach their ends.
Inputs may be any that keep to these rules, and one draw needn't show every extreme that they name: Each row holds 8 lengths that sum to 2048; the longest pair of every pack has exactly 512 tokens.
All inputs are finite; a program needn't handle non-finite values.
Results may differ from the reference program's by a relative error of at most 0.02.
Values may be sent and summed in bfloat16 or wider, within the bound.
A program may use at most 192 MiB of HBM per device.

```python
import math
import jax
import jax.numpy as jnp
import numpy as np
from jax import lax

D = 768
HEADS = 12
HD = 64
FF = 3072
PACK = 2048
MOST = 512
PAIRS = 8
TOKENS = 16384
N_DP = 8
N_TENSOR = 4


def spiked_field(key):
    base_key = jax.random.fold_in(key, 11)
    pair_key = jax.random.fold_in(key, 23)
    values = jnp.clip(jax.random.normal(base_key, (TOKENS, D), jnp.float32), -6.0, 6.0)
    pairing = jax.random.permutation(pair_key, N_DP).astype(jnp.int32)
    row_pack = jnp.arange(TOKENS, dtype=jnp.int32) // PACK
    feature_block = jnp.arange(D, dtype=jnp.int32) // (D // N_DP)
    chosen = pairing[row_pack][:, None] == feature_block[None, :]
    return jnp.where(chosen, 4.0 * values, values)


def draw_tokens(key, part):
    return spiked_field(jax.random.fold_in(key, 101)).astype(jnp.bfloat16)


def draw_cotangent(key, part):
    return spiked_field(jax.random.fold_in(key, 202)).astype(jnp.bfloat16)


def levels(stream_key, shape, shards, smallest, high):
    def one(dim, parts):
        draws = jax.random.uniform(jax.random.fold_in(jax.random.fold_in(stream_key, 6), dim), (parts,), jnp.float32, smallest / len(shards), high / len(shards))
        return jnp.repeat(jnp.exp(draws), shape[dim] // parts).reshape((-1,) + (1,) * (len(shape) - dim - 1))

    level = one(*shards[0])
    for cut in shards[1:]:
        level = level * one(*cut)
    return level


def split_up(count, total, most, skew):
    portions = [(1 << 20) // math.isqrt(grade ** skew) + 1 for grade in range(2, count + 1)]
    spare, given = total - most - (count - 1), [1] * (count - 1)
    while spare > 0:
        free = [i for i in range(count - 1) if given[i] < most]
        whole, left = sum([portions[i] for i in free]), spare
        for i in free:
            more = min(most - given[i], max(1, left * portions[i] // whole), spare)
            given[i] = given[i] + more
            spare = spare - more
    return np.array([most] + given)


def ragged_sizes(rng, count, total, reach, lean):
    if count == 2:
        one = jax.random.randint(rng, (), max(1, total - reach), min(reach, total - 1) + 1)
        return jnp.stack([one, total - one])
    sizes = jnp.asarray(split_up(count, total, reach, lean), jnp.int32)
    pairs = (count - 1) // 2
    source_of, taker = sizes[1:1 + 2 * pairs:2], sizes[2:2 + 2 * pairs:2]
    margin = jnp.minimum(source_of - 1, reach - taker)
    shifted = jax.random.randint(jax.random.fold_in(rng, 1), (pairs,), 0, 1 << 20) % (margin + 1)
    sizes = sizes.at[1:1 + 2 * pairs:2].set(source_of - shifted).at[2:2 + 2 * pairs:2].set(taker + shifted)
    return sizes[jax.random.permutation(jax.random.fold_in(rng, 2), count)]


def normal_values(stream_key, dims, scale, reach, cuts=(), kind=jnp.bfloat16):
    array = scale * jax.random.normal(stream_key, dims, jnp.float32)
    if cuts:
        array = array * levels(stream_key, dims, cuts, -0.22, 0.18)
    return jnp.clip(array, -reach, reach).astype(kind)


def setup_inputs(seed: int = 0) -> dict:
    seeds = jax.random.split(jax.random.key(seed), 16)
    return {
        "tokens": draw_tokens(jax.random.fold_in(seeds[15], 71), 0),
        "lengths": jax.vmap(lambda own: ragged_sizes(own, PAIRS, PACK, MOST, 2))(jax.random.split(seeds[1], N_DP)).reshape((N_DP, PAIRS)).astype(jnp.int32),
        "w_qkv": normal_values(seeds[2], (3, D, D), D ** -0.5, 0.21875, ((2, 4),)),
        "b_qv": normal_values(seeds[3], (2, D), 0.5, 3.0, ((1, 4),)),
        "w_out": normal_values(seeds[4], (D, D), (D // 16) ** -0.5, 0.875, ((0, 4),)),
        "b_out": normal_values(seeds[5], (D,), 0.5, 3.0),
        "ln1_gain": jnp.clip(1.0 + 0.18 * jax.random.normal(seeds[6], (D,), jnp.float32), 0.099609375, 1.8984375).astype(jnp.bfloat16),
        "ln1_bias": normal_values(seeds[7], (D,), 0.5, 3.0),
        "w_up": normal_values(seeds[8], (D, FF), D ** -0.5, 0.21875, ((1, 4),)),
        "b_up": normal_values(seeds[9], (FF,), 0.5, 3.0, ((0, 4),)),
        "w_down": normal_values(seeds[10], (FF, D), FF ** -0.5, 0.109375, ((0, 4),)),
        "b_down": normal_values(seeds[11], (D,), 0.5, 3.0),
        "ln2_gain": jnp.clip(1.0 + 0.18 * jax.random.normal(seeds[12], (D,), jnp.float32), 0.099609375, 1.8984375).astype(jnp.bfloat16),
        "ln2_bias": normal_values(seeds[13], (D,), 0.5, 3.0),
        "cotangent": draw_cotangent(jax.random.fold_in(seeds[15], 71), 0),
    }


epsilon = 1e-05
highest = lax.Precision.HIGHEST

@jax.custom_vjp
def low(v):
    return lax.optimization_barrier(v.astype(jnp.bfloat16)).astype(jnp.float32)

@jax.custom_vjp
def low_back(v):
    return v

def low_keep(v):
    return (low(v), None)

def low_pass(kept, grad):
    return (grad,)

def back_keep(v):
    return (v, None)

def back_low(kept, grad):
    return (low(grad),)
low.defvjp(low_keep, low_pass)
low_back.defvjp(back_keep, back_low)

def segment_ids(pair_lengths, count):
    pair_ends = jnp.cumsum(pair_lengths)
    positions = jnp.arange(count, dtype=jnp.int32)
    return lax.optimization_barrier(jnp.sum((positions[:, None] >= pair_ends[None, :]).astype(jnp.int32), axis=1))

def layer_norm(values, gain, shift_bias):
    average = lax.optimization_barrier(jnp.mean(values, axis=-1, keepdims=True))
    centred = values - average
    inv_spread = lax.rsqrt(lax.optimization_barrier(jnp.mean(centred * centred, axis=-1, keepdims=True)) + epsilon)
    return centred * inv_spread * gain + shift_bias

def pack_forward(inputs, pair_lengths, params):
    w_qkv, b_qv, w_out, b_out, gain_one, bias_one, w_up, b_up, w_down, b_down, gain_two, bias_two = params
    segment = segment_ids(pair_lengths, PACK)
    bias_rows = jnp.stack([b_qv[0], jnp.zeros_like(b_qv[0]), b_qv[1]])
    projected = jnp.einsum('td,cde->cte', inputs, w_qkv, precision=highest) + bias_rows[:, None, :]
    qkv_low = low(low_back(projected))
    padded = jnp.pad(qkv_low[1:], ((0, 0), (MOST, MOST), (0, 0)))
    segment_pad = jnp.pad(segment, (MOST, MOST), constant_values=-1)
    factor = HD ** (-0.5)

    def one_block(block_index):
        offset = block_index * MOST
        queries = lax.dynamic_slice_in_dim(qkv_low[0], offset, MOST, 0).reshape(MOST, HEADS, HD)
        window = lax.dynamic_slice_in_dim(padded, offset, 3 * MOST, 1).reshape(2, 3 * MOST, HEADS, HD)
        query_segment = lax.dynamic_slice_in_dim(segment, offset, MOST, 0)
        key_segment = lax.dynamic_slice_in_dim(segment_pad, offset, 3 * MOST, 0)
        allowed = query_segment[:, None] == key_segment[None, :]
        products = jnp.einsum('qhd,khd->hqk', queries, window[0], precision=highest) * factor
        scores = jnp.where(allowed[None], low_back(products), -1e+30)
        soft_weights = low(jax.nn.softmax(scores, axis=-1))
        context = jnp.einsum('hqk,khd->qhd', soft_weights, window[1], precision=highest)
        return context.reshape(MOST, D)
    context = lax.map(jax.checkpoint(one_block), jnp.arange(PACK // MOST, dtype=jnp.int32))
    context = low(low_back(context.reshape(PACK, D)))
    group_width = D // N_TENSOR
    attn_parts = jnp.einsum('tnc,ncd->ntd', context.reshape(PACK, N_TENSOR, group_width), w_out.reshape(N_TENSOR, group_width, D), precision=highest)
    attended = low_back(lax.optimization_barrier(jnp.sum(low(attn_parts), axis=0)))
    hidden_one = layer_norm(inputs + attended + b_out, gain_one, bias_one)
    pre_act = low_back(jnp.dot(low(hidden_one), w_up, precision=highest) + b_up)
    activated = low(jax.nn.gelu(pre_act, approximate=False))
    unit_width = FF // N_TENSOR
    ffn_parts = jnp.einsum('tnf,nfd->ntd', activated.reshape(PACK, N_TENSOR, unit_width), w_down.reshape(N_TENSOR, unit_width, D), precision=highest)
    fed = low_back(lax.optimization_barrier(jnp.sum(low(ffn_parts), axis=0)))
    return layer_norm(hidden_one + fed + b_down, gain_two, bias_two)

def reference(tokens, lengths, w_qkv, b_qv, w_out, b_out, ln1_gain, ln1_bias, w_up, b_up, w_down, b_down, ln2_gain, ln2_bias, cotangent):
    params = tuple((member.astype(jnp.float32) for member in (w_qkv, b_qv, w_out, b_out, ln1_gain, ln1_bias, w_up, b_up, w_down, b_down, ln2_gain, ln2_bias)))
    inputs = tokens.astype(jnp.float32).reshape(N_DP, PACK, D)

    def forward(values, weights):

        def per_pack(pack_item):
            return pack_forward(pack_item[0], pack_item[1], weights)
        return lax.map(jax.checkpoint(per_pack), (values, lengths))
    outputs, pull = jax.vjp(forward, inputs, params)
    grad_inputs, grads = pull(cotangent.astype(jnp.float32).reshape(N_DP, PACK, D))
    return (outputs.reshape(TOKENS, D).astype(jnp.bfloat16), grad_inputs.reshape(TOKENS, D).astype(jnp.bfloat16), grads[0], grads[1], grads[2], grads[3], grads[4], grads[5], grads[6], grads[7], grads[8], grads[9], grads[10], grads[11])
```

```python
import functools

import jax
import jax.numpy as jnp
from jax import lax
from jax.experimental import pallas as pl
from jax.experimental.pallas import tpu as pltpu
from jax.sharding import PartitionSpec as P

HD = 64
MOST = 512
GROUP = 8
TILE = 256
epsilon = 1e-05
MESH = pl.DeviceIdType.MESH
F32 = jnp.float32
BF16 = jnp.bfloat16


def mm(a, b):
    return lax.dot_general(a, b, (((1,), (0,)), ((), ())), preferred_element_type=F32)


def mm_nt(a, b):
    return lax.dot_general(a, b, (((1,), (1,)), ((), ())), preferred_element_type=F32)


def mm_tn(a, b):
    return lax.dot_general(a, b, (((0,), (0,)), ((), ())), preferred_element_type=F32)


def mm_tt(a, b):
    return lax.dot_general(a, b, (((0,), (1,)), ((), ())), preferred_element_type=F32)


def peers_of(group_rank):
    core = group_rank % 2
    along_x = (group_rank // 2) % 2
    along_y = group_rank // 4
    step_x = 2 - 4 * along_x
    step_y = 4 - 8 * along_y
    return group_rank + 1 - 2 * core, group_rank + step_x, group_rank + step_y, group_rank + step_x + step_y


def greet(devices):
    barrier = pltpu.get_barrier_semaphore()
    for device in devices:
        pl.semaphore_signal(barrier, inc=1, device_id=device, device_id_type=MESH)
    pl.semaphore_wait(barrier, len(devices))


def remote(src, dst, send_sem, recv_sem, device):
    return pltpu.make_async_remote_copy(
        src_ref=src, dst_ref=dst, send_sem=send_sem, recv_sem=recv_sem, device_id=device, device_id_type=MESH
    )


def forward_kernel(
    parts, tok, wqkv, bias, seg_row, seg_col, up, down, out,
    q_t, k_n, v_t, lse, ctx_all, up_all, down_all, out_all,
    k_pad, v_pad, ctx, z_send, z_recv, x_send, x_recv, c_send, c_recv, a_send, a_recv, l_sem,
):
    rows = tok.shape[0]
    width = wqkv.shape[2]
    heads = width // HD
    share = rows // parts
    dp = lax.axis_index("dp")
    me = lax.axis_index("tensor")
    rank = dp % GROUP
    base = dp - rank
    others = peers_of(rank)
    shards = (out, up, down)
    fulls = (out_all, up_all, down_all)

    def at(j):
        return (me + j) % parts

    greet([(dp, at(j)) for j in range(1, parts)] + [(base + other, me) for other in others])

    def z_copy(w, j):
        return remote(
            shards[w].at[rank], fulls[w].at[me, rank], z_send.at[w, j - 1], z_recv.at[w, j - 1], (dp, at(j))
        )

    def x_copy(w, j, k, slot):
        source = at(parts - j)
        piece = fulls[w].at[source, slot]
        return remote(piece, piece, x_send.at[w, j - 1, k], x_recv.at[w, j - 1, k], (base + others[1 + k], me))

    def c_copy(w, j, k, slot):
        source = at(parts - j)
        piece = fulls[w].at[source, slot]
        return remote(piece, piece, c_send.at[w, j - 1, k], c_recv.at[w, j - 1, k], (base + others[0], me))

    for w in range(3):
        for j in range(1, parts):
            z_copy(w, j).start()
    own = [pltpu.make_async_copy(shards[w], fulls[w].at[me], l_sem.at[w]) for w in range(3)]
    for copy in own:
        copy.start()

    def spread(w):
        for j in range(1, parts):
            z_copy(w, j).wait_recv()
            for k in range(3):
                x_copy(w, j, k, rank).start()

    def pass_on(w):
        for j in range(1, parts):
            c_copy(w, j, 0, rank).start()
            for k in range(3):
                x_copy(w, j, k, others[1 + k]).wait_recv()
                c_copy(w, j, 1 + k, others[1 + k]).start()

    k_pad[:, :MOST] = jnp.zeros((heads, MOST, HD), BF16)
    k_pad[:, MOST + rows :] = jnp.zeros((heads, MOST, HD), BF16)
    v_pad[:, :MOST] = jnp.zeros((width, MOST), BF16)
    v_pad[:, MOST + rows :] = jnp.zeros((width, MOST), BF16)

    @pl.loop(0, rows // TILE)
    def _(t):
        here = pl.ds(pl.multiple_of(t * TILE, TILE), TILE)
        there = pl.ds(pl.multiple_of(t * TILE + MOST, TILE), TILE)
        x = tok[here, :]
        q_t[:, here] = (mm_tt(wqkv[0], x) + bias[0]).astype(BF16)
        keys = mm(x, wqkv[1]).astype(BF16)
        k_n[here, :] = keys
        for h in range(heads):
            k_pad[h, there, :] = keys[:, h * HD : (h + 1) * HD]
        values = (mm_tt(wqkv[2], x) + bias[1]).astype(BF16)
        v_t[:, here] = values
        v_pad[:, there] = values

    spread(0)
    span = TILE + 2 * MOST
    per_block = share // TILE
    scale = HD ** (-0.5)

    def a_copy(j):
        block = at(j)
        return remote(ctx.at[block], ctx_all.at[me], a_send.at[j - 1], a_recv.at[j - 1], (dp, block))

    @pl.loop(0, rows // TILE)
    def _(step):
        block = (me + 1 + step // per_block) % parts
        inner = (step % per_block) * TILE
        begin = block * share + inner
        here = pl.ds(pl.multiple_of(begin, TILE), TILE)
        window = pl.ds(pl.multiple_of(begin, TILE), span)
        allowed_q = seg_row[:, here]
        allowed_k = seg_col[window, :]
        allowed = jnp.concatenate(
            [allowed_k == allowed_q[:, i * 128 : (i + 1) * 128] for i in range(TILE // 128)], axis=1
        )
        outs = []
        for h in range(heads):
            hs = pl.ds(h * HD, HD)
            queries = q_t[hs, here] * jnp.asarray(scale, BF16)
            scores = jnp.where(allowed, mm(k_pad[h, window, :], queries), -1e30)
            top = jnp.max(scores, axis=0, keepdims=True)
            weights = jnp.exp(scores - top)
            total = jnp.sum(weights, axis=0, keepdims=True)
            lse[h : h + 1, here] = top + jnp.log(total)
            outs.append(mm(v_pad[hs, window], weights.astype(BF16)) / total)
        result = jnp.concatenate(outs, axis=0).T.astype(BF16)
        ctx[block, pl.ds(pl.multiple_of(inner, TILE), TILE), :] = result
        for j in range(1, parts):

            @pl.when(step == j * per_block)
            def _(j=j):
                a_copy(j).start()

        @pl.when(step == 3)
        def _():
            spread(1)

    keep = pltpu.make_async_copy(ctx.at[me], ctx_all.at[me], l_sem.at[3])
    keep.start()
    spread(2)
    for w in range(3):
        pass_on(w)
    for j in range(1, parts):
        a_copy(j).wait()
    for w in range(3):
        for j in range(1, parts):
            z_copy(w, j).wait_send()
            c_copy(w, j, 0, rank).wait_send()
            c_copy(w, j, 0, others[0]).wait_recv()
            for k in range(3):
                x_copy(w, j, k, rank).wait_send()
                c_copy(w, j, 1 + k, others[1 + k]).wait()
    for copy in own:
        copy.wait()
    keep.wait()


def forward_part(parts, tokens, w_qkv, bias, seg_row, seg_col, w_up, w_down, w_out):
    rows, model = tokens.shape
    width = w_qkv.shape[2]
    heads = width // HD
    share = rows // parts

    def sliced(w):
        return w.reshape(GROUP, w.shape[0] // GROUP, w.shape[1])

    shards = [sliced(w) for w in (w_up, w_down, w_out)]
    vmem = pl.BlockSpec(memory_space=pltpu.VMEM)
    hbm = pl.BlockSpec(memory_space=pl.ANY)
    dma = pltpu.SemaphoreType.DMA
    outs = pl.pallas_call(
        functools.partial(forward_kernel, parts),
        out_shape=[
            jax.ShapeDtypeStruct((width, rows), BF16),
            jax.ShapeDtypeStruct((rows, width), BF16),
            jax.ShapeDtypeStruct((width, rows), BF16),
            jax.ShapeDtypeStruct((heads, rows), F32),
            jax.ShapeDtypeStruct((parts, share, width), BF16),
        ]
        + [jax.ShapeDtypeStruct((parts,) + s.shape, BF16) for s in shards],
        in_specs=[vmem] * 8,
        out_specs=[vmem] * 5 + [hbm] * 3,
        scratch_shapes=[
            pltpu.VMEM((heads, rows + 2 * MOST, HD), BF16),
            pltpu.VMEM((width, rows + 2 * MOST), BF16),
            pltpu.VMEM((parts, share, width), BF16),
            dma((3, parts - 1)),
            dma((3, parts - 1)),
            dma((3, parts - 1, 3)),
            dma((3, parts - 1, 3)),
            dma((3, parts - 1, 4)),
            dma((3, parts - 1, 4)),
            dma((parts - 1,)),
            dma((parts - 1,)),
            dma((4,)),
        ],
        compiler_params=pltpu.CompilerParams(
            collective_id=0, has_side_effects=True, vmem_limit_bytes=60 * 1024 * 1024
        ),
        name="forward_part",
    )(tokens, w_qkv, bias, seg_row, seg_col, *shards)
    q_t, k_n, v_t, lse, ctx_all, up_all, down_all, out_all = outs
    return (
        q_t, k_n, v_t, lse, ctx_all,
        up_all.reshape((parts,) + w_up.shape),
        down_all.reshape((parts,) + w_down.shape),
        out_all.reshape((parts,) + w_out.shape),
    )


def segment_ids(pair_lengths, count):
    pair_ends = jnp.cumsum(pair_lengths)
    positions = jnp.arange(count, dtype=jnp.int32)
    return jnp.sum((positions[:, None] >= pair_ends[None, :]).astype(jnp.int32), axis=1)


def norm_forward(values, gain, shift_bias):
    average = jnp.mean(values, axis=-1, keepdims=True)
    centred = values - average
    inv_spread = lax.rsqrt(jnp.mean(centred * centred, axis=-1, keepdims=True) + epsilon)
    normed = centred * inv_spread
    return (normed * gain + shift_bias, normed, inv_spread)


def norm_backward(upstream, normed, inv_spread, gain):
    scaled = upstream * gain
    adjusted = (
        scaled
        - jnp.mean(scaled, axis=-1, keepdims=True)
        - normed * jnp.mean(scaled * normed, axis=-1, keepdims=True)
    )
    return (adjusted * inv_spread, jnp.sum(upstream * normed, axis=0), jnp.sum(upstream, axis=0))


def gelu_exact(value):
    return jax.nn.gelu(value, approximate=False)


def middle_part(parts, x_own, g_own, ctx_all, w_out, w_up, w_down, b_out, g1, s1, b_up, b_down, g2, s2):
    own, width = ctx_all.shape[1], ctx_all.shape[2]
    model = w_out.shape[2]
    ctx = jnp.transpose(ctx_all, (1, 0, 2)).reshape(own, parts * width)
    out_full = w_out.reshape(parts * width, model)
    mixed_one = x_own + mm(ctx, out_full) + b_out
    hidden_one, normed_one, spread_one = norm_forward(mixed_one, g1, s1)
    low = hidden_one.astype(BF16)
    pre = [mm(low, w_up[n]) + b_up[n] for n in range(parts)]
    act = [gelu_exact(p).astype(BF16) for p in pre]
    fed = sum(mm(act[n], w_down[n]) for n in range(parts))
    mixed_two = hidden_one + fed + b_down
    layer_out, normed_two, spread_two = norm_forward(mixed_two, g2, s2)
    grad_two, gain_two, shift_two = norm_backward(g_own, normed_two, spread_two, g2)
    d_fed = grad_two.astype(BF16)
    grad_down = [mm_tn(d_fed, act[n]) for n in range(parts)]
    d_pre = [jax.vjp(gelu_exact, pre[n])[1](mm_nt(d_fed, w_down[n]))[0].astype(BF16) for n in range(parts)]
    grad_up = [mm_tn(low, d_pre[n]) for n in range(parts)]
    up_bias = jnp.stack([jnp.sum(d.astype(F32), axis=0) for d in d_pre])
    grad_hidden = grad_two + sum(mm_nt(d_pre[n], w_up[n]) for n in range(parts))
    grad_one, gain_one, shift_one = norm_backward(grad_hidden, normed_one, spread_one, g1)
    d_att = grad_one.astype(BF16)
    grad_out = [mm_tn(d_att, ctx_all[n]) for n in range(parts)]
    d_ctx = jnp.stack([mm_nt(d_att, w_out[n]).astype(BF16) for n in range(parts)])
    small = jnp.stack(
        [jnp.sum(grad_one, axis=0), gain_one, shift_one, jnp.sum(grad_two, axis=0), gain_two, shift_two]
    )
    return layer_out.astype(BF16), grad_one, d_ctx, grad_down, grad_up, grad_out, up_bias, small


def per_device(
    tokens,
    lengths,
    w_qkv,
    b_qv,
    w_out,
    b_out,
    ln1_gain,
    ln1_bias,
    w_up,
    b_up,
    w_down,
    b_down,
    ln2_gain,
    ln2_bias,
    cotangent,
):
    rows = tokens.shape[0]
    width = w_out.shape[0]
    heads = width // HD
    parts = lax.axis_size("tensor")
    share = rows // parts
    me = lax.axis_index("tensor")
    segment = segment_ids(lengths[0], rows)
    seg_row = segment[None, :]
    seg_col = jnp.broadcast_to(
        jnp.pad(segment, (MOST, MOST), constant_values=-1)[:, None], (rows + 2 * MOST, 128)
    )
    bias = b_qv.astype(F32)[:, :, None]
    q_t, k_n, v_t, lse, ctx_all, up_full, down_full, out_full = forward_part(
        parts, tokens, w_qkv, bias, seg_row, seg_col, w_up, w_down, w_out
    )
    b_up_full = lax.all_gather(b_up, "tensor").astype(F32)
    x_own = lax.dynamic_slice_in_dim(tokens, me * share, share, 0).astype(F32)
    g_own = lax.dynamic_slice_in_dim(cotangent, me * share, share, 0).astype(F32)
    layer_out, grad_one, d_ctx, grad_down, grad_up, grad_out, up_bias, small = middle_part(
        parts, x_own, g_own, ctx_all, out_full, up_full, down_full,
        b_out.astype(F32), ln1_gain.astype(F32), ln1_bias.astype(F32), b_up_full,
        b_down.astype(F32), ln2_gain.astype(F32), ln2_bias.astype(F32),
    )
    d_ctx_own = lax.all_to_all(d_ctx, "tensor", 0, 0).reshape(rows, width)
    dq, dk, dv = backward_plain(q_t, k_n, v_t, lse, d_ctx_own, segment)
    d_qkv = jnp.stack([dq, dk, dv])
    grad_qkv_t = jnp.einsum("td,cte->dce", tokens, d_qkv, preferred_element_type=F32)
    qkv_bias = jnp.sum(d_qkv.astype(F32), axis=1)
    partial_input = jnp.einsum("cte,cde->td", d_qkv, w_qkv, preferred_element_type=F32)
    input_share = lax.psum_scatter(
        partial_input.astype(BF16), "tensor", scatter_dimension=0, tiled=True
    ).astype(F32)
    input_grad = (input_share + grad_one).astype(BF16)
    bias_grads = lax.psum(jnp.stack([qkv_bias[0], qkv_bias[2]]), "dp")
    up_bias_grad = lax.psum(lax.psum_scatter(up_bias, "tensor", scatter_dimension=0, tiled=True), "dp")[0]
    small_share = lax.psum_scatter(lax.psum(small, "tensor"), "dp", scatter_dimension=1, tiled=True)
    qkv_share = lax.psum_scatter(grad_qkv_t, "dp", scatter_dimension=0, tiled=True)

    def shared(blocks):
        stacked = jnp.stack(blocks).astype(BF16)
        over = lax.psum_scatter(stacked, "dp", scatter_dimension=1, tiled=True)
        return lax.psum_scatter(over, "tensor", scatter_dimension=0, tiled=True)[0].astype(F32)

    return (
        layer_out,
        input_grad,
        jnp.transpose(qkv_share, (1, 0, 2)),
        bias_grads,
        shared(grad_out).T,
        small_share[0],
        small_share[1],
        small_share[2],
        shared(grad_up),
        up_bias_grad,
        shared(grad_down).T,
        small_share[3],
        small_share[4],
        small_share[5],
    )


def backward_plain(q_t, k_n, v_t, lse, d_ctx, segment):
    width, rows = q_t.shape
    heads = width // HD
    queries = q_t.T.reshape(rows, heads, HD)
    keys = k_n.reshape(rows, heads, HD)
    values = v_t.T.reshape(rows, heads, HD)
    upstream = d_ctx.reshape(rows, heads, HD)
    scale = HD ** (-0.5)
    scores = jnp.einsum("qhd,khd->hqk", queries, keys, preferred_element_type=F32) * scale
    scores = jnp.where((segment[:, None] == segment[None, :])[None], scores, -1e30)
    soft = jnp.exp(scores - lse[..., None])
    dv = jnp.einsum("hqk,qhd->khd", soft.astype(BF16), upstream, preferred_element_type=F32)
    dp = jnp.einsum("qhd,khd->hqk", upstream, values, preferred_element_type=F32)
    ds = (soft * (dp - jnp.sum(dp * soft, axis=-1, keepdims=True))).astype(BF16)
    dq = jnp.einsum("hqk,khd->qhd", ds, keys, preferred_element_type=F32) * scale
    dk = jnp.einsum("hqk,qhd->khd", ds, queries, preferred_element_type=F32) * scale
    return tuple(d.reshape(rows, width).astype(BF16) for d in (dq, dk, dv))


def solution(mesh):
    return jax.shard_map(
        per_device,
        mesh=mesh,
        in_specs=(
            P("dp", None),
            P("dp", None),
            P(None, None, "tensor"),
            P(None, "tensor"),
            P("tensor", None),
            P(),
            P(),
            P(),
            P(None, "tensor"),
            P("tensor"),
            P("tensor", None),
            P(),
            P(),
            P(),
            P("dp", None),
        ),
        out_specs=(
            P(("dp", "tensor"), None),
            P(("dp", "tensor"), None),
            P(None, "dp", "tensor"),
            P(None, "tensor"),
            P("tensor", "dp"),
            P("dp"),
            P("dp"),
            P("dp"),
            P("dp", "tensor"),
            P("tensor"),
            P("tensor", "dp"),
            P("dp"),
            P("dp"),
            P("dp"),
        ),
        check_vma=False,
    )
```

```python
import functools

import jax
import jax.numpy as jnp
from jax import lax
from jax.experimental import pallas as pl
from jax.experimental.pallas import tpu as pltpu
from jax.sharding import PartitionSpec as P

HD = 64
MOST = 512
GROUP = 8
TILE = 256
epsilon = 1e-05
MESH = pl.DeviceIdType.MESH
F32 = jnp.float32
BF16 = jnp.bfloat16


def mm(a, b):
    return lax.dot_general(a, b, (((1,), (0,)), ((), ())), preferred_element_type=F32)


def mm_nt(a, b):
    return lax.dot_general(a, b, (((1,), (1,)), ((), ())), preferred_element_type=F32)


def mm_tn(a, b):
    return lax.dot_general(a, b, (((0,), (0,)), ((), ())), preferred_element_type=F32)


def mm_tt(a, b):
    return lax.dot_general(a, b, (((0,), (1,)), ((), ())), preferred_element_type=F32)


def peers_of(group_rank):
    core = group_rank % 2
    along_x = (group_rank // 2) % 2
    along_y = group_rank // 4
    step_x = 2 - 4 * along_x
    step_y = 4 - 8 * along_y
    return group_rank + 1 - 2 * core, group_rank + step_x, group_rank + step_y, group_rank + step_x + step_y


def greet(devices):
    barrier = pltpu.get_barrier_semaphore()
    for device in devices:
        pl.semaphore_signal(barrier, inc=1, device_id=device, device_id_type=MESH)
    pl.semaphore_wait(barrier, len(devices))


def remote(src, dst, send_sem, recv_sem, device):
    return pltpu.make_async_remote_copy(
        src_ref=src, dst_ref=dst, send_sem=send_sem, recv_sem=recv_sem, device_id=device, device_id_type=MESH
    )


def forward_kernel(
    parts, tok, wqkv, bias, seg_row, seg_col, b_up, up, down, out,
    q_t, k_n, v_t, lse, ctx_all, b_all, up_all, down_all, out_all,
    k_pad, v_pad, ctx, z_send, z_recv, x_send, x_recv, c_send, c_recv, a_send, a_recv, b_send, b_recv, l_sem,
):
    rows = tok.shape[0]
    width = wqkv.shape[2]
    heads = width // HD
    share = rows // parts
    dp = lax.axis_index("dp")
    me = lax.axis_index("tensor")
    rank = dp % GROUP
    base = dp - rank
    others = peers_of(rank)
    shards = (out, up, down)
    fulls = (out_all, up_all, down_all)

    def at(j):
        return (me + j) % parts

    greet([(dp, at(j)) for j in range(1, parts)] + [(base + other, me) for other in others])

    def z_copy(w, j):
        return remote(
            shards[w].at[rank], fulls[w].at[me, rank], z_send.at[w, j - 1], z_recv.at[w, j - 1], (dp, at(j))
        )

    def x_copy(w, j, k, slot, to):
        piece = fulls[w].at[at(parts - j), slot]
        return remote(piece, piece, x_send.at[w, j - 1, k], x_recv.at[w, j - 1, k], (base + to, me))

    through = (1, 1, 2)

    def c_copy(w, j, k, slot):
        source = at(parts - j)
        piece = fulls[w].at[source, slot]
        return remote(piece, piece, c_send.at[w, j - 1, k], c_recv.at[w, j - 1, k], (base + others[0], me))

    def b_copy(j):
        return remote(b_up, b_all.at[me], b_send.at[j - 1], b_recv.at[j - 1], (dp, at(j)))

    for j in range(1, parts):
        b_copy(j).start()
    for w in range(3):
        for j in range(1, parts):
            z_copy(w, j).start()
    b_all[me] = b_up[...]
    own = [pltpu.make_async_copy(shards[w], fulls[w].at[me], l_sem.at[w]) for w in range(3)]
    for copy in own:
        copy.start()

    def spread(w):
        for j in range(1, parts):
            z_copy(w, j).wait_recv()
            for k in (1, 2):
                x_copy(w, j, k, rank, others[k]).start()

    def relay(w):
        k = through[w]
        for j in range(1, parts):
            x_copy(w, j, k, others[k], others[k]).wait_recv()
            x_copy(w, j, 0, others[k], others[3 - k]).start()
            c_copy(w, j, 0, rank).start()
            c_copy(w, j, k, others[k]).start()

    def pass_on(w):
        k = 3 - through[w]
        for j in range(1, parts):
            x_copy(w, j, k, others[k], others[k]).wait_recv()
            c_copy(w, j, k, others[k]).start()
        for j in range(1, parts):
            x_copy(w, j, 0, others[3], others[k]).wait_recv()
            c_copy(w, j, 3, others[3]).start()

    k_pad[:, :MOST] = jnp.zeros((heads, MOST, HD), BF16)
    k_pad[:, MOST + rows :] = jnp.zeros((heads, MOST, HD), BF16)
    v_pad[:, :MOST] = jnp.zeros((width, MOST), BF16)
    v_pad[:, MOST + rows :] = jnp.zeros((width, MOST), BF16)

    @pl.loop(0, rows // TILE)
    def _(t):
        here = pl.ds(pl.multiple_of(t * TILE, TILE), TILE)
        there = pl.ds(pl.multiple_of(t * TILE + MOST, TILE), TILE)
        x = tok[here, :]
        q_t[:, here] = (mm_tt(wqkv[0], x) + bias[0]).astype(BF16)
        keys = mm(x, wqkv[1]).astype(BF16)
        k_n[here, :] = keys
        for h in range(heads):
            k_pad[h, there, :] = keys[:, h * HD : (h + 1) * HD]
        values = (mm_tt(wqkv[2], x) + bias[1]).astype(BF16)
        v_t[:, here] = values
        v_pad[:, there] = values

    spread(0)
    span = TILE + 2 * MOST
    per_block = share // TILE
    scale = HD ** (-0.5)

    def a_copy(j):
        block = at(j)
        return remote(ctx.at[block], ctx_all.at[me], a_send.at[j - 1], a_recv.at[j - 1], (dp, block))

    @pl.loop(0, rows // TILE)
    def _(step):
        block = (me + 1 + step // per_block) % parts
        inner = (step % per_block) * TILE
        begin = block * share + inner
        here = pl.ds(pl.multiple_of(begin, TILE), TILE)
        window = pl.ds(pl.multiple_of(begin, TILE), span)
        allowed_q = seg_row[:, here]
        allowed_k = seg_col[window, :]
        allowed = jnp.concatenate(
            [allowed_k == allowed_q[:, i * 128 : (i + 1) * 128] for i in range(TILE // 128)], axis=1
        )
        outs = []
        for h in range(heads):
            hs = pl.ds(h * HD, HD)
            queries = q_t[hs, here] * jnp.asarray(scale, BF16)
            scores = jnp.where(allowed, mm(k_pad[h, window, :], queries), -1e30)
            top = jnp.max(scores, axis=0, keepdims=True)
            weights = jnp.exp(scores - top)
            total = jnp.sum(weights, axis=0, keepdims=True)
            lse[h : h + 1, here] = top + jnp.log(total)
            outs.append(mm(v_pad[hs, window], weights.astype(BF16)) / total)
        result = jnp.concatenate(outs, axis=0).T.astype(BF16)
        ctx[block, pl.ds(pl.multiple_of(inner, TILE), TILE), :] = result
        for j in range(1, parts):

            @pl.when(step == j * per_block)
            def _(j=j):
                a_copy(j).start()

        for when, what, w in ((0, relay, 0), (1, spread, 1), (4, spread, 2), (5, relay, 1), (6, pass_on, 0)):

            @pl.when(step == when)
            def _(what=what, w=w):
                what(w)

    keep = pltpu.make_async_copy(ctx.at[me], ctx_all.at[me], l_sem.at[3])
    keep.start()
    relay(2)
    pass_on(1)
    pass_on(2)
    for j in range(1, parts):
        a_copy(j).wait()
        b_copy(j).wait()
    for w in range(3):
        for j in range(1, parts):
            z_copy(w, j).wait_send()
            for k in (1, 2):
                x_copy(w, j, k, rank, others[k]).wait_send()
            x_copy(w, j, 0, others[3], others[3 - through[w]]).wait_send()
            for k in range(4):
                c_copy(w, j, k, others[0]).wait()
    for copy in own:
        copy.wait()
    keep.wait()


def forward_part(parts, tokens, w_qkv, bias, seg_row, seg_col, b_up, w_up, w_down, w_out):
    rows, model = tokens.shape
    width = w_qkv.shape[2]
    heads = width // HD
    share = rows // parts

    def sliced(w):
        return w.reshape(GROUP, w.shape[0] // GROUP, w.shape[1])

    shards = [sliced(w) for w in (w_up, w_down, w_out)]
    vmem = pl.BlockSpec(memory_space=pltpu.VMEM)
    hbm = pl.BlockSpec(memory_space=pl.ANY)
    dma = pltpu.SemaphoreType.DMA
    outs = pl.pallas_call(
        functools.partial(forward_kernel, parts),
        out_shape=[
            jax.ShapeDtypeStruct((width, rows), BF16),
            jax.ShapeDtypeStruct((rows, width), BF16),
            jax.ShapeDtypeStruct((width, rows), BF16),
            jax.ShapeDtypeStruct((heads, rows), F32),
            jax.ShapeDtypeStruct((parts, share, width), BF16),
            jax.ShapeDtypeStruct((parts,) + b_up.shape, F32),
        ]
        + [jax.ShapeDtypeStruct((parts,) + s.shape, BF16) for s in shards],
        in_specs=[vmem] * 9,
        out_specs=[vmem] * 6 + [hbm] * 3,
        scratch_shapes=[
            pltpu.VMEM((heads, rows + 2 * MOST, HD), BF16),
            pltpu.VMEM((width, rows + 2 * MOST), BF16),
            pltpu.VMEM((parts, share, width), BF16),
            dma((3, parts - 1)),
            dma((3, parts - 1)),
            dma((3, parts - 1, 3)),
            dma((3, parts - 1, 3)),
            dma((3, parts - 1, 4)),
            dma((3, parts - 1, 4)),
            dma((parts - 1,)),
            dma((parts - 1,)),
            dma((parts - 1,)),
            dma((parts - 1,)),
            dma((4,)),
        ],
        compiler_params=pltpu.CompilerParams(
            collective_id=0, has_side_effects=True, vmem_limit_bytes=60 * 1024 * 1024
        ),
        name="forward_part",
    )(tokens, w_qkv, bias, seg_row, seg_col, b_up, *shards)
    q_t, k_n, v_t, lse, ctx_all, b_all, up_all, down_all, out_all = outs
    return (
        q_t, k_n, v_t, lse, ctx_all, b_all[:, 0],
        up_all.reshape((parts,) + w_up.shape),
        down_all.reshape((parts,) + w_down.shape),
        out_all.reshape((parts,) + w_out.shape),
    )


def backward_kernel(
    parts, d_ctx, q_t, k_n, v_t, lse, seg_row, seg_col, tok, wqkv, g_own, sums, g_down, g_up, g_out,
    d_in, s_down, s_up, s_out, s_qkv, s_sums,
    dc, k_pad, v_pad, k_t, q_n, acc_k, acc_v, dq_t, dk, dv, part, chain,
    p_down, p_up, p_out, r_down, r_up, r_out, x_down, x_up, x_out, z_down, z_up, z_out,
    gq, r_gq, x_gq, sum_z, sum_dp, sum_in,
    a_send, a_recv, l_sem, s1_send, s1_recv, s2_send, s2_recv, s3_send, s3_recv,
    h_send, h_recv, m_send, m_recv, n_send, n_recv,
):
    rows, model = tok.shape
    width = wqkv.shape[2]
    heads = width // HD
    share = rows // parts
    dp = lax.axis_index("dp")
    me = lax.axis_index("tensor")
    rank = dp % GROUP
    base = dp - rank
    core = rank % 2
    chip = rank // 2
    others = peers_of(rank)
    full = (g_down, g_up, g_out)
    held = (p_down, p_up, p_out, gq)
    first = (r_down, r_up, r_out, r_gq)
    second = (x_down, x_up, x_out, x_gq)
    third = (z_down, z_up, z_out)
    shared = (s_down, s_up, s_out)
    scale = HD ** (-0.5)

    def at(j):
        return (me + j) % parts

    fellows = [(rank + k) % GROUP for k in range(1, GROUP)]
    greet([(dp, at(j)) for j in range(1, parts)] + [(base + f, me) for f in fellows])

    def a_copy(j):
        return remote(d_ctx.at[at(j)], dc.at[me], a_send.at[j - 1], a_recv.at[j - 1], (dp, at(j)))

    def s1_copy(w):
        src = full[w].at[:, :, 1 - core] if w < 3 else gq.at[:, 1 - core]
        return remote(src, first[w], s1_send.at[w], s1_recv.at[w], (base + others[0], me))

    def s2_copy(w, k):
        to = others[1 + k]
        src = held[w].at[:, to // 2] if w < 3 else gq.at[to // 2, core]
        return remote(src, second[w].at[k], s2_send.at[w, k], s2_recv.at[w, k], (base + to, me))

    def s3_copy(w, j):
        return remote(
            held[w].at[at(j), chip], third[w].at[j - 1], s3_send.at[w, j - 1], s3_recv.at[w, j - 1], (dp, at(j))
        )

    def m_copy(j):
        return remote(sums, sum_z.at[j - 1], m_send.at[j - 1], m_recv.at[j - 1], (dp, at(j)))

    def n_copy(k):
        return remote(sum_in, sum_dp.at[k], n_send.at[k], n_recv.at[k], (base + fellows[k], me))

    for j in range(1, parts):
        a_copy(j).start()
    for j in range(1, parts):
        m_copy(j).start()
    loads = [pltpu.make_async_copy(full[w].at[:, :, core], held[w], l_sem.at[w]) for w in range(3)]
    for w in range(3):
        s1_copy(w).start()
        loads[w].start()
    mine = pltpu.make_async_copy(d_ctx.at[me], dc.at[me], l_sem.at[3])
    mine.start()

    for ref in (k_pad, v_pad):
        ref[:MOST, :] = jnp.zeros((MOST, width), BF16)
        ref[MOST + rows :, :] = jnp.zeros((MOST, width), BF16)
    k_t[:, :MOST] = jnp.zeros((width, MOST), BF16)
    k_t[:, MOST + rows :] = jnp.zeros((width, MOST), BF16)

    @pl.loop(0, rows // TILE)
    def _(t):
        here = pl.ds(pl.multiple_of(t * TILE, TILE), TILE)
        there = pl.ds(pl.multiple_of(t * TILE + MOST, TILE), TILE)
        keys = k_n[here, :]
        k_pad[there, :] = keys
        k_t[:, there] = keys.astype(F32).T.astype(BF16)
        v_pad[there, :] = v_t[:, here].astype(F32).T.astype(BF16)
        q_n[here, :] = (q_t[:, here].astype(F32) * scale).T.astype(BF16)

    @pl.loop(0, (rows + 2 * MOST) // TILE)
    def _(t):
        here = pl.ds(pl.multiple_of(t * TILE, TILE), TILE)
        acc_k[here, :] = jnp.zeros((TILE, width), F32)
        acc_v[here, :] = jnp.zeros((TILE, width), F32)

    def s1_finish(w):
        s1_copy(w).wait_recv()
        loads[w].wait()

        @pl.loop(0, parts)
        def _(n):
            for c in range(GROUP // 2):
                held[w][n, c] = (held[w][n, c].astype(F32) + first[w][n, c].astype(F32)).astype(BF16)

        for k in range(3):
            s2_copy(w, k).start()

    def s2_finish(w):
        for k in range(3):
            s2_copy(w, k).wait_recv()

        @pl.loop(0, parts)
        def _(n):
            total = held[w][n, chip].astype(F32)
            for k in range(3):
                total = total + second[w][k, n].astype(F32)
            held[w][n, chip] = total.astype(BF16)

        for j in range(1, parts):
            s3_copy(w, j).start()

    def s3_finish(w):
        for j in range(1, parts):
            s3_copy(w, j).wait_recv()
        total = held[w][me, chip].astype(F32)
        for j in range(1, parts):
            total = total + third[w][j - 1].astype(F32)
        shared[w][...] = total

    span = TILE + 2 * MOST
    per_block = share // TILE
    mine.wait()

    @pl.loop(0, rows // TILE)
    def _(step):
        for j in range(1, parts):

            @pl.when(step == j * per_block)
            def _(j=j):
                a_copy(parts - j).wait_recv()

        block = (me + step // per_block) % parts
        inner = (step % per_block) * TILE
        begin = block * share + inner
        here = pl.ds(pl.multiple_of(begin, TILE), TILE)
        window = pl.ds(pl.multiple_of(begin, TILE), span)
        allowed_q = seg_row[:, here]
        allowed_k = seg_col[window, :]
        allowed = jnp.concatenate(
            [allowed_k == allowed_q[:, i * 128 : (i + 1) * 128] for i in range(TILE // 128)], axis=1
        )
        up_n = dc[block, pl.ds(pl.multiple_of(inner, TILE), TILE), :]
        up_t = up_n.astype(F32).T.astype(BF16)
        grads_k = []
        grads_v = []
        for h in range(heads):
            hs = slice(h * HD, (h + 1) * HD)
            queries = q_t[hs, here] * jnp.asarray(scale, BF16)
            scores = jnp.where(allowed, mm(k_pad[window, :][:, hs], queries), -1e30)
            soft = jnp.exp(scores - lse[h : h + 1, here])
            grad = mm(v_pad[window, :][:, hs], up_t[hs, :])
            shift = jnp.sum(grad * soft, axis=0, keepdims=True)
            inner_grad = (soft * (grad - shift)).astype(BF16)
            grads_v.append(mm(soft.astype(BF16), up_n[:, hs]))
            grads_k.append(mm(inner_grad, q_n[here, :][:, hs]))
            dq_t[hs, here] = (mm(k_t[hs, window], inner_grad) * scale).astype(BF16)
        acc_k[window, :] += jnp.concatenate(grads_k, axis=1)
        acc_v[window, :] += jnp.concatenate(grads_v, axis=1)

        @pl.when(step == 1)
        def _():
            s1_finish(0)

        @pl.when(step == 3)
        def _():
            s1_finish(1)

        @pl.when(step == 4)
        def _():
            s1_finish(2)

        @pl.when(step == 6)
        def _():
            s2_finish(0)

    @pl.loop(0, rows // TILE)
    def _(t):
        here = pl.ds(pl.multiple_of(t * TILE, TILE), TILE)
        there = pl.ds(pl.multiple_of(t * TILE + MOST, TILE), TILE)
        dk[here, :] = acc_k[there, :].astype(BF16)
        dv[here, :] = acc_v[there, :].astype(BF16)

    def own_part(b):
        @pl.loop(0, per_block)
        def _(t):
            here = pl.ds(pl.multiple_of(b * share + t * TILE, TILE), TILE)
            total = mm_tt(dq_t[:, here], wqkv[0]) + mm_nt(dk[here, :], wqkv[1]) + mm_nt(dv[here, :], wqkv[2])
            part[b, pl.ds(pl.multiple_of(t * TILE, TILE), TILE), :] = total.astype(BF16)

    def right_copy(b):
        return remote(part.at[b], chain.at[b], h_send.at[0, b], h_recv.at[0, b], (dp, me + 1))

    def left_copy(b):
        slot = jnp.where(b == me - 1, parts, b)
        return remote(part.at[b], chain.at[slot], h_send.at[1, b], h_recv.at[1, b], (dp, me - 1))

    def fold(b):
        @pl.loop(0, per_block)
        def _(t):
            here = pl.ds(pl.multiple_of(t * TILE, TILE), TILE)
            part[b, here, :] = (part[b, here, :].astype(F32) + chain[b, here, :].astype(F32)).astype(BF16)

    def go_right(b):
        @pl.when(me < b)
        def _():
            @pl.when(me > 0)
            def _():
                right_copy(b).wait_recv()
                fold(b)

            right_copy(b).start()

    def go_left(b):
        @pl.when(me > b)
        def _():
            @pl.when(me < parts - 1)
            def _():
                remote(part.at[b], chain.at[b], h_send.at[1, b], h_recv.at[1, b], (dp, me - 1)).wait_recv()
                fold(b)

            left_copy(b).start()

    own_part(parts - 1)
    own_part(0)
    go_right(parts - 1)
    go_left(0)
    for b in range(parts - 2, 0, -1):
        own_part(b)
    s2_finish(1)

    for c in range(3):
        if c == 0:
            grads = mm(dq_t[...], tok[...])
        else:
            grads = mm_tn((dk, dv)[c - 1][...], tok[...])
        grads = grads.T.astype(BF16)
        deep = model // GROUP
        for i in range(GROUP):
            gq[i // 2, i % 2, c] = grads[i * deep : (i + 1) * deep, :]
    remote(gq.at[:, 1 - core], r_gq, s1_send.at[3], s1_recv.at[3], (base + others[0], me)).start()
    for j in range(1, parts):
        m_copy(j).wait_recv()
    total = sums[...]
    for j in range(1, parts):
        total = total + sum_z[j - 1]
    sum_in[...] = total
    keep = sum_in.shape[0] - 8
    flat_q = jnp.sum(dq_t[...].astype(F32), axis=1, keepdims=True).T
    flat_v = jnp.sum(dv[...].astype(F32), axis=0, keepdims=True)
    sum_in[keep : keep + 1, :width] = flat_q
    sum_in[keep + 1 : keep + 2, :width] = flat_v
    for k in range(GROUP - 1):
        n_copy(k).start()

    go_right(parts - 2)
    go_left(1)
    s1_copy(3).wait_recv()
    for c in range(GROUP // 2):
        for i in range(3):
            gq[c, core, i] = (gq[c, core, i].astype(F32) + r_gq[c, i].astype(F32)).astype(BF16)
    for k in range(3):
        s2_copy(3, k).start()
    s2_finish(2)
    for b in range(parts - 3, 0, -1):
        go_right(b)
    for b in range(2, parts - 1):
        go_left(b)

    for k in range(3):
        s2_copy(3, k).wait_recv()
    for i in range(3):
        block = gq[chip, core, i].astype(F32)
        for k in range(3):
            block = block + x_gq[k, i].astype(F32)
        s_qkv[i] = block
    for k in range(GROUP - 1):
        n_copy(k).wait()
    total = sum_in[...]
    for k in range(GROUP - 1):
        total = total + sum_dp[k]
    s_sums[...] = total
    for w in range(3):
        s3_finish(w)

    @pl.when(me > 0)
    def _():
        remote(part.at[me], chain.at[me], h_send.at[0, me], h_recv.at[0, me], (dp, me)).wait_recv()
        fold(me)

    @pl.when(me < parts - 1)
    def _():
        remote(part.at[me], chain.at[parts], h_send.at[1, me], h_recv.at[1, me], (dp, me)).wait_recv()

        @pl.loop(0, per_block)
        def _(t):
            here = pl.ds(pl.multiple_of(t * TILE, TILE), TILE)
            part[me, here, :] = (part[me, here, :].astype(F32) + chain[parts, here, :].astype(F32)).astype(BF16)

    @pl.loop(0, per_block)
    def _(t):
        here = pl.ds(pl.multiple_of(t * TILE, TILE), TILE)
        d_in[here, :] = (part[me, here, :].astype(F32) + g_own[here, :]).astype(BF16)

    for j in range(1, parts):
        a_copy(j).wait_send()
        m_copy(j).wait_send()
    for w in range(4):
        s1_copy(w).wait_send()
        for k in range(3):
            s2_copy(w, k).wait_send()
    for w in range(3):
        for j in range(1, parts):
            s3_copy(w, j).wait_send()
    for b in range(1, parts):

        @pl.when(me < b)
        def _(b=b):
            right_copy(b).wait_send()

    for b in range(parts - 1):

        @pl.when(me > b)
        def _(b=b):
            left_copy(b).wait_send()


def backward_part(parts, d_ctx, q_t, k_n, v_t, lse, seg_row, seg_col, tokens, w_qkv, g_own, sums, grads):
    rows, model = tokens.shape
    width = w_qkv.shape[2]
    heads = width // HD
    share = rows // parts
    deep = model // GROUP
    wides = [g.shape[2] for g in grads]
    blocks = [g.reshape(parts, GROUP // 2, 2, deep, g.shape[2]) for g in grads]
    vmem = pl.BlockSpec(memory_space=pltpu.VMEM)
    hbm = pl.BlockSpec(memory_space=pl.ANY)
    dma = pltpu.SemaphoreType.DMA
    padded = rows + 2 * MOST

    def held(*lead):
        return [pltpu.VMEM(lead + (deep, w), BF16) for w in wides]

    return pl.pallas_call(
        functools.partial(backward_kernel, parts),
        out_shape=[jax.ShapeDtypeStruct((share, model), BF16)]
        + [jax.ShapeDtypeStruct((deep, w), F32) for w in wides]
        + [jax.ShapeDtypeStruct((3, deep, width), F32), jax.ShapeDtypeStruct(sums.shape, F32)],
        in_specs=[vmem] * 11 + [hbm] * 3,
        out_specs=[vmem] * 6,
        scratch_shapes=[
            pltpu.VMEM((parts, share, width), BF16),
            pltpu.VMEM((padded, width), BF16),
            pltpu.VMEM((padded, width), BF16),
            pltpu.VMEM((width, padded), BF16),
            pltpu.VMEM((rows, width), BF16),
            pltpu.VMEM((padded, width), F32),
            pltpu.VMEM((padded, width), F32),
            pltpu.VMEM((width, rows), BF16),
            pltpu.VMEM((rows, width), BF16),
            pltpu.VMEM((rows, width), BF16),
            pltpu.VMEM((parts, share, model), BF16),
            pltpu.VMEM((parts + 1, share, model), BF16),
        ]
        + held(parts, GROUP // 2)
        + held(parts, GROUP // 2)
        + held(3, parts)
        + held(parts - 1)
        + [
            pltpu.VMEM((GROUP // 2, 2, 3, deep, width), BF16),
            pltpu.VMEM((GROUP // 2, 3, deep, width), BF16),
            pltpu.VMEM((3, 3, deep, width), BF16),
            pltpu.VMEM((parts - 1,) + sums.shape, F32),
            pltpu.VMEM((GROUP - 1,) + sums.shape, F32),
            pltpu.VMEM(sums.shape, F32),
            dma((parts - 1,)),
            dma((parts - 1,)),
            dma((4,)),
            dma((4,)),
            dma((4,)),
            dma((4, 3)),
            dma((4, 3)),
            dma((3, parts - 1)),
            dma((3, parts - 1)),
            dma((2, parts)),
            dma((2, parts)),
            dma((parts - 1,)),
            dma((parts - 1,)),
            dma((GROUP - 1,)),
            dma((GROUP - 1,)),
        ],
        compiler_params=pltpu.CompilerParams(
            collective_id=1, has_side_effects=True, vmem_limit_bytes=64 * 1024 * 1024 - 128 * 1024
        ),
        name="backward_part",
    )(d_ctx, q_t, k_n, v_t, lse, seg_row, seg_col, tokens, w_qkv, g_own, sums, *blocks)


def segment_ids(pair_lengths, count):
    pair_ends = jnp.cumsum(pair_lengths)
    positions = jnp.arange(count, dtype=jnp.int32)
    return jnp.sum((positions[:, None] >= pair_ends[None, :]).astype(jnp.int32), axis=1)


def norm_forward(values, gain, shift_bias):
    average = jnp.mean(values, axis=-1, keepdims=True)
    centred = values - average
    inv_spread = lax.rsqrt(jnp.mean(centred * centred, axis=-1, keepdims=True) + epsilon)
    normed = centred * inv_spread
    return (normed * gain + shift_bias, normed, inv_spread)


def middle_kernel(
    parts, x, g, ctx, vecs, b_up, out_hbm, up_hbm, down_hbm,
    layer_out, grad_one, d_ctx, sums, g_down, g_up, g_out,
    out, up, down, act, slope, low, low_t, hid, normed, inv, fed, d_fed, d_fed_t, d_pre,
    v_down, v_up, v_out, l_sem, s_sem,
):
    own, model = x.shape
    half = own // 2
    loads = [
        pltpu.make_async_copy(a.at[n], b.at[n], l_sem.at[i, n])
        for i, (a, b) in enumerate(((out_hbm, out), (up_hbm, up), (down_hbm, down)))
        for n in range(parts)
    ]
    for load in loads:
        load.start()
    b_out, g1, s1, b_down, g2, s2 = [vecs[i : i + 1, :] for i in range(6)]
    sums[...] = jnp.zeros(sums.shape, F32)
    for load in loads[:parts]:
        load.wait()

    def rows_of(r):
        return pl.ds(pl.multiple_of(r * half, half), half)

    def add_to(row, values):
        sums[row : row + 1, :] += jnp.sum(values, axis=0, keepdims=True)

    @pl.loop(0, 2)
    def _(r):
        here = rows_of(r)
        mixed = x[here, :].astype(F32) + b_out
        for n in range(parts):
            mixed = mixed + mm(ctx[n, here, :], out[n])
        value, n1, r1 = norm_forward(mixed, g1, s1)
        hid[here, :] = value
        normed[here, :] = n1
        inv[here, :] = jnp.broadcast_to(r1, (half, 128))
        low[here, :] = value.astype(BF16)
        low_t[:, here] = value.T.astype(BF16)
        fed[here, :] = value + b_down

    for load in loads[parts:]:
        load.wait()

    @pl.loop(0, parts * 2)
    def _(t):
        n = t // 2
        here = rows_of(t % 2)
        pre = mm(low[here, :], up[n]) + b_up[pl.ds(n, 1), :]
        share = 0.5 + 0.5 * lax.erf(pre * (0.5**0.5))
        slope[n, here, :] = share + pre * (jnp.exp(-0.5 * pre * pre) * 0.3989422804014327)
        value = (pre * share).astype(BF16)
        act[n, here, :] = value
        fed[here, :] += mm(value, down[n])

    @pl.loop(0, 2)
    def _(r):
        here = rows_of(r)
        value, n2, r2 = norm_forward(fed[here, :], g2, s2)
        layer_out[here, :] = value.astype(BF16)
        cot = g[here, :].astype(F32)
        scaled = cot * g2
        grad_two = (
            scaled
            - jnp.mean(scaled, axis=-1, keepdims=True)
            - n2 * jnp.mean(scaled * n2, axis=-1, keepdims=True)
        ) * r2
        add_to(3, grad_two)
        add_to(4, cot * n2)
        add_to(5, cot)
        fed[here, :] = grad_two
        d_fed[here, :] = grad_two.astype(BF16)
        d_fed_t[:, here] = grad_two.T.astype(BF16)

    def store(which, n):
        src, dst = ((v_down, g_down), (v_up, g_up), (v_out, g_out))[which]
        return pltpu.make_async_copy(src.at[n], dst.at[n], s_sem.at[which, n])

    @pl.loop(0, parts)
    def _(n):
        v_down[n] = mm(d_fed_t[...], act[n]).astype(BF16)
        store(0, n).start()

        @pl.loop(0, 2)
        def _(r):
            here = rows_of(r)
            grad = (mm_nt(d_fed[here, :], down[n]) * slope[n, here, :]).astype(BF16)
            d_pre[here, :] = grad
            sums[pl.ds(8 + n, 1), :] += jnp.sum(grad.astype(F32), axis=0, keepdims=True)
            fed[here, :] += mm_nt(grad, up[n])

        v_up[n] = mm(low_t[...], d_pre[...]).astype(BF16)
        store(1, n).start()

    @pl.loop(0, 2)
    def _(r):
        here = rows_of(r)
        n1 = normed[here, :]
        grad = fed[here, :]
        scaled = grad * g1
        value = (
            scaled
            - jnp.mean(scaled, axis=-1, keepdims=True)
            - n1 * jnp.mean(scaled * n1, axis=-1, keepdims=True)
        ) * inv[here, 0:1]
        add_to(0, value)
        add_to(1, grad * n1)
        add_to(2, grad)
        grad_one[here, :] = value
        d_fed_t[:, here] = value.T.astype(BF16)
        d_att = value.astype(BF16)
        for n in range(parts):
            d_ctx[n, here, :] = mm_nt(d_att, out[n]).astype(BF16)

    @pl.loop(0, parts)
    def _(n):
        v_out[n] = mm(d_fed_t[...], ctx[n]).astype(BF16)
        store(2, n).start()

    for which in range(3):
        for n in range(parts):
            store(which, n).wait()


def middle_part(parts, x_own, g_own, ctx_all, w_out, w_up, w_down, vecs, b_up):
    own, width = ctx_all.shape[1], ctx_all.shape[2]
    model = w_out.shape[2]
    units = w_up.shape[2]
    vmem = pl.BlockSpec(memory_space=pltpu.VMEM)
    hbm = pl.BlockSpec(memory_space=pl.ANY)
    grads = [(parts, model, units), (parts, model, units), (parts, model, width)]
    return pl.pallas_call(
        functools.partial(middle_kernel, parts),
        out_shape=[
            jax.ShapeDtypeStruct((own, model), BF16),
            jax.ShapeDtypeStruct((own, model), F32),
            jax.ShapeDtypeStruct(ctx_all.shape, BF16),
            jax.ShapeDtypeStruct((24, model), F32),
        ]
        + [jax.ShapeDtypeStruct(shape, BF16) for shape in grads],
        in_specs=[vmem] * 5 + [hbm] * 3,
        out_specs=[vmem] * 4 + [hbm] * 3,
        scratch_shapes=[
            pltpu.VMEM(w_out.shape, BF16),
            pltpu.VMEM(w_up.shape, BF16),
            pltpu.VMEM(w_down.shape, BF16),
            pltpu.VMEM((parts, own, units), BF16),
            pltpu.VMEM((parts, own, units), F32),
            pltpu.VMEM((own, model), BF16),
            pltpu.VMEM((model, own), BF16),
            pltpu.VMEM((own, model), F32),
            pltpu.VMEM((own, model), F32),
            pltpu.VMEM((own, 128), F32),
            pltpu.VMEM((own, model), F32),
            pltpu.VMEM((own, model), BF16),
            pltpu.VMEM((model, own), BF16),
            pltpu.VMEM((own, units), BF16),
        ]
        + [pltpu.VMEM(shape, BF16) for shape in grads]
        + [pltpu.SemaphoreType.DMA((3, parts))] * 2,
        compiler_params=pltpu.CompilerParams(vmem_limit_bytes=60 * 1024 * 1024),
        name="middle_part",
    )(x_own, g_own, ctx_all, vecs, b_up, w_out, w_up, w_down)


def per_device(
    tokens,
    lengths,
    w_qkv,
    b_qv,
    w_out,
    b_out,
    ln1_gain,
    ln1_bias,
    w_up,
    b_up,
    w_down,
    b_down,
    ln2_gain,
    ln2_bias,
    cotangent,
):
    rows = tokens.shape[0]
    width = w_out.shape[0]
    heads = width // HD
    parts = lax.axis_size("tensor")
    share = rows // parts
    me = lax.axis_index("tensor")
    segment = segment_ids(lengths[0], rows)
    seg_row = segment[None, :]
    seg_col = jnp.broadcast_to(
        jnp.pad(segment, (MOST, MOST), constant_values=-1)[:, None], (rows + 2 * MOST, 128)
    )
    bias = b_qv.astype(F32)[:, :, None]
    b_up_rows = jnp.broadcast_to(b_up.astype(F32)[None], (8, b_up.shape[0]))
    q_t, k_n, v_t, lse, ctx_all, b_up_full, up_full, down_full, out_full = forward_part(
        parts, tokens, w_qkv, bias, seg_row, seg_col, b_up_rows, w_up, w_down, w_out
    )
    x_own = lax.dynamic_slice_in_dim(tokens, me * share, share, 0)
    g_own = lax.dynamic_slice_in_dim(cotangent, me * share, share, 0)
    blank = jnp.zeros_like(b_out)
    vecs = jnp.stack([b_out, ln1_gain, ln1_bias, b_down, ln2_gain, ln2_bias, blank, blank]).astype(F32)
    layer_out, grad_one, d_ctx, sums, grad_down, grad_up, grad_out = middle_part(
        parts, x_own, g_own, ctx_all, out_full, up_full, down_full, vecs, b_up_full
    )
    if lax.axis_size("dp") == GROUP:
        grads = [grad_down, grad_up, grad_out]
        d_in, s_down, s_up, s_out, s_qkv, s_sums = backward_part(
            parts, d_ctx, q_t, k_n, v_t, lse, seg_row, seg_col, tokens, w_qkv, grad_one, sums, grads
        )
        deep = sums.shape[1] // GROUP
        own = lax.dynamic_slice_in_dim(s_sums, lax.axis_index("dp") * deep, deep, 1)
        return (
            layer_out,
            d_in,
            s_qkv,
            s_sums[16:18, :width],
            s_out.T,
            own[0],
            own[1],
            own[2],
            s_up,
            lax.dynamic_index_in_dim(s_sums, 8 + me, 0, keepdims=False),
            s_down.T,
            own[3],
            own[4],
            own[5],
        )
    small, up_bias = sums[:6], sums[8 : 8 + parts]
    d_ctx_own = lax.all_to_all(d_ctx, "tensor", 0, 0).reshape(rows, width)
    dq, dk, dv = backward_plain(q_t, k_n, v_t, lse, d_ctx_own, segment)
    d_qkv = jnp.stack([dq, dk, dv])
    grad_qkv_t = jnp.einsum("td,cte->dce", tokens, d_qkv, preferred_element_type=F32)
    qkv_bias = jnp.sum(d_qkv.astype(F32), axis=1)
    partial_input = jnp.einsum("cte,cde->td", d_qkv, w_qkv, preferred_element_type=F32)
    input_share = lax.psum_scatter(
        partial_input.astype(BF16), "tensor", scatter_dimension=0, tiled=True
    ).astype(F32)
    input_grad = (input_share + grad_one).astype(BF16)
    bias_grads = lax.psum(jnp.stack([qkv_bias[0], qkv_bias[2]]), "dp")
    up_bias_grad = lax.psum(lax.psum_scatter(up_bias, "tensor", scatter_dimension=0, tiled=True), "dp")[0]
    small_share = lax.psum_scatter(lax.psum(small, "tensor"), "dp", scatter_dimension=1, tiled=True)
    qkv_share = lax.psum_scatter(grad_qkv_t, "dp", scatter_dimension=0, tiled=True)

    def shared(blocks):
        over = lax.psum_scatter(blocks, "dp", scatter_dimension=1, tiled=True)
        return lax.psum_scatter(over, "tensor", scatter_dimension=0, tiled=True)[0].astype(F32)

    return (
        layer_out,
        input_grad,
        jnp.transpose(qkv_share, (1, 0, 2)),
        bias_grads,
        shared(grad_out).T,
        small_share[0],
        small_share[1],
        small_share[2],
        shared(grad_up),
        up_bias_grad,
        shared(grad_down).T,
        small_share[3],
        small_share[4],
        small_share[5],
    )


def backward_plain(q_t, k_n, v_t, lse, d_ctx, segment):
    width, rows = q_t.shape
    heads = width // HD
    queries = q_t.T.reshape(rows, heads, HD)
    keys = k_n.reshape(rows, heads, HD)
    values = v_t.T.reshape(rows, heads, HD)
    upstream = d_ctx.reshape(rows, heads, HD)
    scale = HD ** (-0.5)
    scores = jnp.einsum("qhd,khd->hqk", queries, keys, preferred_element_type=F32) * scale
    scores = jnp.where((segment[:, None] == segment[None, :])[None], scores, -1e30)
    soft = jnp.exp(scores - lse[..., None])
    dv = jnp.einsum("hqk,qhd->khd", soft.astype(BF16), upstream, preferred_element_type=F32)
    dp = jnp.einsum("qhd,khd->hqk", upstream, values, preferred_element_type=F32)
    ds = (soft * (dp - jnp.sum(dp * soft, axis=-1, keepdims=True))).astype(BF16)
    dq = jnp.einsum("hqk,khd->qhd", ds, keys, preferred_element_type=F32) * scale
    dk = jnp.einsum("hqk,qhd->khd", ds, queries, preferred_element_type=F32) * scale
    return tuple(d.reshape(rows, width).astype(BF16) for d in (dq, dk, dv))


def solution(mesh):
    return jax.shard_map(
        per_device,
        mesh=mesh,
        in_specs=(
            P("dp", None),
            P("dp", None),
            P(None, None, "tensor"),
            P(None, "tensor"),
            P("tensor", None),
            P(),
            P(),
            P(),
            P(None, "tensor"),
            P("tensor"),
            P("tensor", None),
            P(),
            P(),
            P(),
            P("dp", None),
        ),
        out_specs=(
            P(("dp", "tensor"), None),
            P(("dp", "tensor"), None),
            P(None, "dp", "tensor"),
            P(None, "tensor"),
            P("tensor", "dp"),
            P("dp"),
            P("dp"),
            P("dp"),
            P("dp", "tensor"),
            P("tensor"),
            P("tensor", "dp"),
            P("dp"),
            P("dp"),
            P("dp"),
        ),
        check_vma=False,
    )
```

```python
import functools

import jax
import jax.numpy as jnp
from jax import lax
from jax.experimental import pallas as pl
from jax.experimental.pallas import tpu as pltpu
from jax.sharding import PartitionSpec as P

HD = 64
MOST = 512
GROUP = 8
TILE = 256
epsilon = 1e-05
MESH = pl.DeviceIdType.MESH
F32 = jnp.float32
BF16 = jnp.bfloat16


def mm(a, b):
    return lax.dot_general(a, b, (((1,), (0,)), ((), ())), preferred_element_type=F32)


def mm_nt(a, b):
    return lax.dot_general(a, b, (((1,), (1,)), ((), ())), preferred_element_type=F32)


def mm_tn(a, b):
    return lax.dot_general(a, b, (((0,), (0,)), ((), ())), preferred_element_type=F32)


def mm_tt(a, b):
    return lax.dot_general(a, b, (((0,), (1,)), ((), ())), preferred_element_type=F32)


def peers_of(group_rank):
    core = group_rank % 2
    along_x = (group_rank // 2) % 2
    along_y = group_rank // 4
    step_x = 2 - 4 * along_x
    step_y = 4 - 8 * along_y
    return group_rank + 1 - 2 * core, group_rank + step_x, group_rank + step_y, group_rank + step_x + step_y


def greet(devices):
    barrier = pltpu.get_barrier_semaphore()
    for device in devices:
        pl.semaphore_signal(barrier, inc=1, device_id=device, device_id_type=MESH)
    pl.semaphore_wait(barrier, len(devices))


def remote(src, dst, send_sem, recv_sem, device):
    return pltpu.make_async_remote_copy(
        src_ref=src, dst_ref=dst, send_sem=send_sem, recv_sem=recv_sem, device_id=device, device_id_type=MESH
    )


def forward_kernel(
    parts, tok, wqkv, bias, seg_row, ends, b_up, up, down, out,
    q_t, k_n, v_t, lse, seg_col, ctx_all, b_all, up_all, down_all, out_all,
    k_pad, v_pad, ctx, z_send, z_recv, x_send, x_recv, c_send, c_recv, a_send, a_recv, b_send, b_recv, l_sem,
):
    rows = tok.shape[0]
    width = wqkv.shape[1]
    heads = width // HD
    share = rows // parts
    dp = lax.axis_index("dp")
    me = lax.axis_index("tensor")
    rank = dp % GROUP
    base = dp - rank
    others = peers_of(rank)
    shards = (out, up, down)
    fulls = (out_all, up_all, down_all)

    def at(j):
        return (me + j) % parts

    greet([(dp, at(j)) for j in range(1, parts)] + [(base + other, me) for other in others])

    def z_copy(w, j):
        return remote(
            shards[w].at[rank], fulls[w].at[me, rank], z_send.at[w, j - 1], z_recv.at[w, j - 1], (dp, at(j))
        )

    def x_copy(w, j, k, slot, to):
        piece = fulls[w].at[at(parts - j), slot]
        return remote(piece, piece, x_send.at[w, j - 1, k], x_recv.at[w, j - 1, k], (base + to, me))

    through = (1, 1, 2)

    def c_copy(w, j, k, slot):
        source = at(parts - j)
        piece = fulls[w].at[source, slot]
        return remote(piece, piece, c_send.at[w, j - 1, k], c_recv.at[w, j - 1, k], (base + others[0], me))

    def b_copy(j):
        return remote(b_up, b_all.at[me], b_send.at[j - 1], b_recv.at[j - 1], (dp, at(j)))

    for j in range(1, parts):
        b_copy(j).start()
    for w in range(3):
        for j in range(1, parts):
            z_copy(w, j).start()
    b_all[me] = b_up[...]
    own = [pltpu.make_async_copy(shards[w], fulls[w].at[me], l_sem.at[w]) for w in range(3)]
    for copy in own:
        copy.start()

    def spread(w):
        for j in range(1, parts):
            z_copy(w, j).wait_recv()
            for k in (1, 2):
                x_copy(w, j, k, rank, others[k]).start()

    def relay(w):
        k = through[w]
        for j in range(1, parts):
            x_copy(w, j, k, others[k], others[k]).wait_recv()
            x_copy(w, j, 0, others[k], others[3 - k]).start()
            c_copy(w, j, 0, rank).start()
            c_copy(w, j, k, others[k]).start()

    def pass_on(w):
        k = 3 - through[w]
        for j in range(1, parts):
            x_copy(w, j, k, others[k], others[k]).wait_recv()
            c_copy(w, j, k, others[k]).start()
        for j in range(1, parts):
            x_copy(w, j, 0, others[3], others[k]).wait_recv()
            c_copy(w, j, 3, others[3]).start()

    k_pad[:, :MOST] = jnp.zeros((heads, MOST, HD), BF16)
    k_pad[:, MOST + rows :] = jnp.zeros((heads, MOST, HD), BF16)
    v_pad[:, :MOST] = jnp.zeros((width, MOST), BF16)
    v_pad[:, MOST + rows :] = jnp.zeros((width, MOST), BF16)

    @pl.loop(0, rows // TILE)
    def _(t):
        here = pl.ds(pl.multiple_of(t * TILE, TILE), TILE)
        there = pl.ds(pl.multiple_of(t * TILE + MOST, TILE), TILE)
        x = tok[here, :]
        q_t[:, here] = (mm_nt(wqkv[0], x) + bias[0]).astype(BF16)
        keys = mm_nt(x, wqkv[1]).astype(BF16)
        k_n[here, :] = keys
        for h in range(heads):
            k_pad[h, there, :] = keys[:, h * HD : (h + 1) * HD]
        values = (mm_nt(wqkv[2], x) + bias[1]).astype(BF16)
        v_t[:, here] = values
        v_pad[:, there] = values

    spread(0)

    @pl.loop(0, (rows + 2 * MOST) // TILE)
    def _(t):
        spot = lax.broadcasted_iota(jnp.int32, (TILE, 128), 0) + (t * TILE - MOST)
        number = jnp.zeros((TILE, 128), jnp.int32)
        for i in range(ends.shape[0]):
            number = number + (spot >= ends[i : i + 1, :]).astype(jnp.int32)
        seg_col[pl.ds(pl.multiple_of(t * TILE, TILE), TILE), :] = jnp.where(spot < 0, -1, number)

    span = TILE + 2 * MOST
    per_block = share // TILE
    scale = HD ** (-0.5)

    def a_copy(j):
        block = at(j)
        return remote(ctx.at[block], ctx_all.at[me], a_send.at[j - 1], a_recv.at[j - 1], (dp, block))

    @pl.loop(0, rows // TILE)
    def _(step):
        block = (me + 1 + step // per_block) % parts
        inner = (step % per_block) * TILE
        begin = block * share + inner
        here = pl.ds(pl.multiple_of(begin, TILE), TILE)
        window = pl.ds(pl.multiple_of(begin, TILE), span)
        allowed_q = seg_row[:, here]
        allowed_k = seg_col[window, :]
        allowed = jnp.concatenate(
            [allowed_k == allowed_q[:, i * 128 : (i + 1) * 128] for i in range(TILE // 128)], axis=1
        )
        outs = []
        for h in range(heads):
            hs = pl.ds(h * HD, HD)
            queries = q_t[hs, here] * jnp.asarray(scale, BF16)
            scores = jnp.where(allowed, mm(k_pad[h, window, :], queries), -1e30)
            top = jnp.max(scores, axis=0, keepdims=True)
            weights = jnp.exp(scores - top)
            total = jnp.sum(weights, axis=0, keepdims=True)
            lse[h : h + 1, here] = top + jnp.log(total)
            outs.append(mm(v_pad[hs, window], weights.astype(BF16)) / total)
        result = jnp.concatenate(outs, axis=0).T.astype(BF16)
        ctx[block, pl.ds(pl.multiple_of(inner, TILE), TILE), :] = result
        for j in range(1, parts):

            @pl.when(step == j * per_block)
            def _(j=j):
                a_copy(j).start()

        for when, what, w in ((0, relay, 0), (1, spread, 1), (4, spread, 2), (5, relay, 1), (6, pass_on, 0)):

            @pl.when(step == when)
            def _(what=what, w=w):
                what(w)

    keep = pltpu.make_async_copy(ctx.at[me], ctx_all.at[me], l_sem.at[3])
    keep.start()
    relay(2)
    pass_on(1)
    pass_on(2)
    for j in range(1, parts):
        a_copy(j).wait()
        b_copy(j).wait()
    for w in range(3):
        for j in range(1, parts):
            z_copy(w, j).wait_send()
            for k in (1, 2):
                x_copy(w, j, k, rank, others[k]).wait_send()
            x_copy(w, j, 0, others[3], others[3 - through[w]]).wait_send()
            for k in range(4):
                c_copy(w, j, k, others[0]).wait()
    for copy in own:
        copy.wait()
    keep.wait()


def forward_part(parts, tokens, w_qkv, bias, seg_row, ends, b_up, w_up, w_down, w_out):
    rows, model = tokens.shape
    width = w_qkv.shape[1]
    heads = width // HD
    share = rows // parts

    def sliced(w):
        return w.reshape(GROUP, w.shape[0] // GROUP, w.shape[1])

    shards = [sliced(w) for w in (w_up, w_down, w_out)]
    vmem = pl.BlockSpec(memory_space=pltpu.VMEM)
    hbm = pl.BlockSpec(memory_space=pl.ANY)
    dma = pltpu.SemaphoreType.DMA
    outs = pl.pallas_call(
        functools.partial(forward_kernel, parts),
        out_shape=[
            jax.ShapeDtypeStruct((width, rows), BF16),
            jax.ShapeDtypeStruct((rows, width), BF16),
            jax.ShapeDtypeStruct((width, rows), BF16),
            jax.ShapeDtypeStruct((heads, rows), F32),
            jax.ShapeDtypeStruct((rows + 2 * MOST, 128), jnp.int32),
            jax.ShapeDtypeStruct((parts, share, width), BF16),
            jax.ShapeDtypeStruct((parts,) + b_up.shape, F32),
        ]
        + [jax.ShapeDtypeStruct((parts,) + s.shape, BF16) for s in shards],
        in_specs=[vmem] * 9,
        out_specs=[vmem] * 7 + [hbm] * 3,
        scratch_shapes=[
            pltpu.VMEM((heads, rows + 2 * MOST, HD), BF16),
            pltpu.VMEM((width, rows + 2 * MOST), BF16),
            pltpu.VMEM((parts, share, width), BF16),
            dma((3, parts - 1)),
            dma((3, parts - 1)),
            dma((3, parts - 1, 3)),
            dma((3, parts - 1, 3)),
            dma((3, parts - 1, 4)),
            dma((3, parts - 1, 4)),
            dma((parts - 1,)),
            dma((parts - 1,)),
            dma((parts - 1,)),
            dma((parts - 1,)),
            dma((4,)),
        ],
        compiler_params=pltpu.CompilerParams(
            collective_id=0, has_side_effects=True, vmem_limit_bytes=60 * 1024 * 1024
        ),
        name="forward_part",
    )(tokens, w_qkv, bias, seg_row, ends, b_up, *shards)
    q_t, k_n, v_t, lse, seg_col, ctx_all, b_all, up_all, down_all, out_all = outs
    return (
        q_t, k_n, v_t, lse, seg_col, ctx_all, b_all[:, 0],
        up_all.reshape((parts,) + w_up.shape),
        down_all.reshape((parts,) + w_down.shape),
        out_all.reshape((parts,) + w_out.shape),
    )


def backward_kernel(
    parts, d_ctx, q_t, k_n, v_t, lse, seg_row, seg_col, tok, g_own, sums, w_hbm, g_down, g_up, g_out,
    d_in, s_down, s_up, s_out, s_qkv, s_sums,
    dc, k_pad, v_pad, k_t, q_n, acc_k, acc_v, pq, pk, rq, rk, w_all,
    p_down, p_up, p_out, r_down, r_up, r_out, x_down, x_up, x_out, y_down, y_up, y_out, z_down, z_up, z_out,
    gq, r_gq, x_gq, sum_z, sum_dp, sum_in,
    a_send, a_recv, l_sem, s1_send, s1_recv, s2_send, s2_recv, s3_send, s3_recv,
    e_send, e_recv, h_send, h_recv, m_send, m_recv, n_send, n_recv,
):
    rows, model = tok.shape
    width = q_t.shape[0]
    heads = width // HD
    share = rows // parts
    dp = lax.axis_index("dp")
    me = lax.axis_index("tensor")
    rank = dp % GROUP
    base = dp - rank
    core = rank % 2
    chip = rank // 2
    along_y, along_x = chip // 2, chip % 2
    others = peers_of(rank)
    starts = (2, 1, 2)
    full = (g_down, g_up, g_out)
    held = (p_down, p_up, p_out, gq)
    first = (r_down, r_up, r_out, r_gq)
    second = (x_down, x_up, x_out)
    last = (y_down, y_up, y_out)
    third = (z_down, z_up, z_out)
    shared = (s_down, s_up, s_out)
    scale = HD ** (-0.5)

    def at(j):
        return (me + j) % parts

    fellows = [(rank + k) % GROUP for k in range(1, GROUP)]
    greet([(dp, at(j)) for j in range(1, parts)] + [(base + f, me) for f in fellows])

    def order(k):
        return jnp.where(me < parts // 2, (me + k) % parts, (me + parts - k) % parts)

    def a_copy(to):
        return remote(d_ctx.at[to], dc.at[me], a_send.at[to], a_recv.at[me], (dp, to))

    def a_wait(source):
        remote(d_ctx.at[source], dc.at[source], a_send.at[source], a_recv.at[source], (dp, source)).wait_recv()

    def s1_copy(w):
        src = full[w].at[:, :, :, 1 - core] if w < 3 else gq.at[:, 1 - core]
        return remote(src, first[w], s1_send.at[w], s1_recv.at[w], (base + others[0], me))

    def s2_copy(w):
        if starts[w] == 1:
            src = held[w].at[:, :, 1 - along_x]
        else:
            src = held[w].at[:, 1 - along_y]
        return remote(src, second[w], s2_send.at[w, 0], s2_recv.at[w, 0], (base + others[starts[w]], me))

    def s2_then(w):
        if starts[w] == 1:
            src = held[w].at[:, 1 - along_y, along_x]
        else:
            src = held[w].at[:, along_y, 1 - along_x]
        return remote(src, last[w], s2_send.at[w, 1], s2_recv.at[w, 1], (base + others[3 - starts[w]], me))

    def gq_copy(k):
        to = others[1 + k]
        return remote(gq.at[to // 2, core], x_gq.at[k], s2_send.at[3, k], s2_recv.at[3, k], (base + to, me))

    def s3_copy(w, j):
        return remote(
            held[w].at[at(j), along_y, along_x],
            third[w].at[j - 1],
            s3_send.at[w, j - 1],
            s3_recv.at[w, j - 1],
            (dp, at(j)),
        )

    def m_copy(j):
        return remote(sums, sum_z.at[j - 1], m_send.at[j - 1], m_recv.at[j - 1], (dp, at(j)))

    def n_copy(k):
        return remote(sum_in, sum_dp.at[k], n_send.at[k], n_recv.at[k], (base + fellows[k], me))

    for k in range(1, parts):
        a_copy(order(k)).start()
    for j in range(1, parts):
        m_copy(j).start()
    loads = [pltpu.make_async_copy(full[w].at[:, :, :, core], held[w], l_sem.at[w]) for w in range(3)]
    for w in range(3):
        s1_copy(w).start()
        loads[w].start()
    mine = pltpu.make_async_copy(d_ctx.at[me], dc.at[me], l_sem.at[3])
    mine.start()
    whole = pltpu.make_async_copy(w_hbm, w_all, l_sem.at[4])
    whole.start()

    for ref in (k_pad, v_pad):
        ref[:MOST, :] = jnp.zeros((MOST, width), BF16)
        ref[MOST + rows :, :] = jnp.zeros((MOST, width), BF16)
    k_t[:, :MOST] = jnp.zeros((width, MOST), BF16)
    k_t[:, MOST + rows :] = jnp.zeros((width, MOST), BF16)

    @pl.loop(0, rows // TILE)
    def _(t):
        here = pl.ds(pl.multiple_of(t * TILE, TILE), TILE)
        there = pl.ds(pl.multiple_of(t * TILE + MOST, TILE), TILE)
        keys = k_n[here, :]
        k_pad[there, :] = keys
        k_t[:, there] = keys.astype(F32).T.astype(BF16)
        v_pad[there, :] = v_t[:, here].astype(F32).T.astype(BF16)
        q_n[here, :] = (q_t[:, here].astype(F32) * scale).T.astype(BF16)

    @pl.loop(0, (rows + 2 * MOST) // TILE)
    def _(t):
        here = pl.ds(pl.multiple_of(t * TILE, TILE), TILE)
        acc_k[here, :] = jnp.zeros((TILE, width), F32)
        acc_v[here, :] = jnp.zeros((TILE, width), F32)

    def s1_finish(w):
        s1_copy(w).wait_recv()
        loads[w].wait()

        @pl.loop(0, parts)
        def _(n):
            for c in range(GROUP // 2):
                at_c = (n, c // 2, c % 2)
                held[w][at_c] = (held[w][at_c].astype(F32) + first[w][at_c].astype(F32)).astype(BF16)

        s2_copy(w).start()

    def s2_finish(w):
        s2_copy(w).wait_recv()

        @pl.loop(0, parts)
        def _(n):
            for c in range(2):
                at_c = (n, c, along_x) if starts[w] == 1 else (n, along_y, c)
                held[w][at_c] = (held[w][at_c].astype(F32) + second[w][n, c].astype(F32)).astype(BF16)

        s2_then(w).start()

    def s2_end(w):
        s2_then(w).wait_recv()

        @pl.loop(0, parts)
        def _(n):
            here = (n, along_y, along_x)
            held[w][here] = (held[w][here].astype(F32) + last[w][n].astype(F32)).astype(BF16)

        for j in range(1, parts):
            s3_copy(w, j).start()

    def s3_finish(w):
        for j in range(1, parts):
            s3_copy(w, j).wait_recv()
        total = held[w][me, along_y, along_x].astype(F32)
        for j in range(1, parts):
            total = total + third[w][j - 1].astype(F32)
        shared[w][...] = total

    span = TILE + 2 * MOST
    per_block = share // TILE
    mine.wait()

    def tile(block, inner):
        begin = block * share + inner
        here = pl.ds(pl.multiple_of(begin, TILE), TILE)
        window = pl.ds(pl.multiple_of(begin, TILE), span)
        allowed_q = seg_row[:, here]
        allowed_k = seg_col[window, :]
        allowed = jnp.concatenate(
            [allowed_k == allowed_q[:, i * 128 : (i + 1) * 128] for i in range(TILE // 128)], axis=1
        )
        up_n = dc[block, pl.ds(pl.multiple_of(inner, TILE), TILE), :]
        up_t = up_n.astype(F32).T.astype(BF16)
        grads_k = []
        grads_v = []
        for h in range(heads):
            hs = slice(h * HD, (h + 1) * HD)
            queries = q_t[hs, here] * jnp.asarray(scale, BF16)
            scores = jnp.where(allowed, mm(k_pad[window, :][:, hs], queries), -1e30)
            soft = jnp.exp(scores - lse[h : h + 1, here])
            grad = mm(v_pad[window, :][:, hs], up_t[hs, :])
            shift = jnp.sum(grad * soft, axis=0, keepdims=True)
            inner_grad = (soft * (grad - shift)).astype(BF16)
            grads_v.append(mm(soft.astype(BF16), up_n[:, hs]))
            grads_k.append(mm(inner_grad, q_n[here, :][:, hs]))
            grad_q = (mm(k_t[hs, window], inner_grad) * scale).astype(BF16)
            pq[block, hs, pl.ds(pl.multiple_of(inner, TILE), TILE)] = grad_q
        acc_k[window, :] += jnp.concatenate(grads_k, axis=1)
        acc_v[window, :] += jnp.concatenate(grads_v, axis=1)

    def q_copy(b):
        return remote(pq.at[b], rq.at[me], e_send.at[b], e_recv.at[me], (dp, b))

    def k_copy(b):
        return remote(pk.at[b], rk.at[me], h_send.at[b], h_recv.at[me], (dp, b))

    def e_wait(m):
        remote(pq.at[m], rq.at[m], e_send.at[m], e_recv.at[m], (dp, m)).wait_recv()
        remote(pk.at[m], rk.at[m], h_send.at[m], h_recv.at[m], (dp, m)).wait_recv()

    def finish(b):
        @pl.loop(0, per_block)
        def _(t):
            there = pl.ds(pl.multiple_of(b * share + t * TILE + MOST, TILE), TILE)
            pair = jnp.concatenate([acc_k[there, :], acc_v[there, :]], axis=1)
            pk[b, pl.ds(pl.multiple_of(t * TILE, TILE), TILE), :] = pair.astype(BF16)

        @pl.when(b != me)
        def _():
            q_copy(b).start()
            k_copy(b).start()

    final = order(parts - 1)
    s1_finish(0)
    s1_finish(1)

    @pl.loop(0, parts)
    def _(k):
        block = order(k)

        @pl.when(k > 0)
        def _():
            a_wait(block)

        @pl.loop(0, per_block)
        def _(t):
            tile(block, t * TILE)

        for when, what, w in ((0, s1_finish, 2),):

            @pl.when(k == when)
            def _(what=what, w=w):
                what(w)

        @pl.when(k >= parts - 2)
        def _():
            @pl.loop(0, parts)
            def _(b):
                early = (b - final >= 2) | (final - b >= 2)

                @pl.when(early == (k == parts - 2))
                def _():
                    finish(b)

    keep_q = pltpu.make_async_copy(pq.at[me], rq.at[me], l_sem.at[5])
    keep_k = pltpu.make_async_copy(pk.at[me], rk.at[me], l_sem.at[6])
    keep_q.start()
    keep_k.start()
    s2_finish(0)

    deep = model // GROUP
    rows_b = [slice(b * share, (b + 1) * share) for b in range(parts)]
    grads_q = sum(mm(pq[b], tok[rows_b[b], :]) for b in range(parts))
    grads_kv = sum(mm_tn(pk[b], tok[rows_b[b], :]) for b in range(parts))
    for c, grads in enumerate((grads_q, grads_kv[:width], grads_kv[width:])):
        grads = grads.T.astype(BF16)
        for i in range(GROUP):
            gq[i // 2, i % 2, c] = grads[i * deep : (i + 1) * deep, :]
    s1_copy(3).start()
    s2_finish(1)
    for j in range(1, parts):
        m_copy(j).wait_recv()
    total = sums[...]
    for j in range(1, parts):
        total = total + sum_z[j - 1]
    sum_in[...] = total
    keep = sum_in.shape[0] - 8
    flat_q = sum(jnp.sum(pq[b].astype(F32), axis=1, keepdims=True) for b in range(parts)).T
    flat_v = sum(jnp.sum(pk[b].astype(F32), axis=0, keepdims=True) for b in range(parts))[:, width:]
    sum_in[keep : keep + 1, :width] = flat_q
    sum_in[keep + 1 : keep + 2, :width] = flat_v
    for k in range(GROUP - 1):
        n_copy(k).start()

    s1_copy(3).wait_recv()
    for c in range(GROUP // 2):
        for i in range(3):
            gq[c, core, i] = (gq[c, core, i].astype(F32) + r_gq[c, i].astype(F32)).astype(BF16)
    s2_finish(2)
    for k in range(3):
        gq_copy(k).start()
    s2_end(0)
    s2_end(1)
    s2_end(2)
    whole.wait()
    keep_q.wait()
    keep_k.wait()
    for j in range(1, parts):
        e_wait(at(j))

    @pl.loop(0, per_block)
    def _(t):
        here = pl.ds(pl.multiple_of(t * TILE, TILE), TILE)
        total = g_own[here, :]
        for m in range(parts):
            pair = rk[m, here, :]
            total = total + mm_tn(rq[m, :, here], w_all[m, 0])
            total = total + mm(pair[:, :width], w_all[m, 1]) + mm(pair[:, width:], w_all[m, 2])
        d_in[here, :] = total.astype(BF16)

    for k in range(3):
        gq_copy(k).wait_recv()
    for i in range(3):
        block = gq[chip, core, i].astype(F32)
        for k in range(3):
            block = block + x_gq[k, i].astype(F32)
        s_qkv[i] = block
    for k in range(GROUP - 1):
        n_copy(k).wait()
    total = sum_in[...]
    for k in range(GROUP - 1):
        total = total + sum_dp[k]
    s_sums[...] = total
    for w in range(3):
        s3_finish(w)

    for k in range(1, parts):
        a_copy(order(k)).wait_send()
        q_copy(order(k)).wait_send()
        k_copy(order(k)).wait_send()

    for j in range(1, parts):
        m_copy(j).wait_send()
    for w in range(4):
        s1_copy(w).wait_send()
    for w in range(3):
        gq_copy(w).wait_send()
        s2_copy(w).wait_send()
        s2_then(w).wait_send()
    for w in range(3):
        for j in range(1, parts):
            s3_copy(w, j).wait_send()


def backward_part(parts, d_ctx, q_t, k_n, v_t, lse, seg_row, seg_col, tokens, qkv_full, g_own, sums, grads):
    rows, model = tokens.shape
    width = q_t.shape[0]
    heads = width // HD
    share = rows // parts
    deep = model // GROUP
    wides = [g.shape[2] for g in grads]
    blocks = [g.reshape(parts, 2, 2, 2, deep, g.shape[2]) for g in grads]
    vmem = pl.BlockSpec(memory_space=pltpu.VMEM)
    hbm = pl.BlockSpec(memory_space=pl.ANY)
    dma = pltpu.SemaphoreType.DMA
    padded = rows + 2 * MOST

    def held(*lead):
        return [pltpu.VMEM(lead + (deep, w), BF16) for w in wides]

    return pl.pallas_call(
        functools.partial(backward_kernel, parts),
        out_shape=[jax.ShapeDtypeStruct((share, model), BF16)]
        + [jax.ShapeDtypeStruct((deep, w), F32) for w in wides]
        + [jax.ShapeDtypeStruct((3, deep, width), F32), jax.ShapeDtypeStruct(sums.shape, F32)],
        in_specs=[vmem] * 10 + [hbm] * 4,
        out_specs=[vmem] * 6,
        scratch_shapes=[
            pltpu.VMEM((parts, share, width), BF16),
            pltpu.VMEM((padded, width), BF16),
            pltpu.VMEM((padded, width), BF16),
            pltpu.VMEM((width, padded), BF16),
            pltpu.VMEM((rows, width), BF16),
            pltpu.VMEM((padded, width), F32),
            pltpu.VMEM((padded, width), F32),
            pltpu.VMEM((parts, width, share), BF16),
            pltpu.VMEM((parts, share, 2 * width), BF16),
            pltpu.VMEM((parts, width, share), BF16),
            pltpu.VMEM((parts, share, 2 * width), BF16),
            pltpu.VMEM(qkv_full.shape, BF16),
        ]
        + held(parts, 2, 2)
        + held(parts, 2, 2)
        + held(parts, 2)
        + held(parts)
        + held(parts - 1)
        + [
            pltpu.VMEM((GROUP // 2, 2, 3, deep, width), BF16),
            pltpu.VMEM((GROUP // 2, 3, deep, width), BF16),
            pltpu.VMEM((3, 3, deep, width), BF16),
            pltpu.VMEM((parts - 1,) + sums.shape, F32),
            pltpu.VMEM((GROUP - 1,) + sums.shape, F32),
            pltpu.VMEM(sums.shape, F32),
            dma((parts,)),
            dma((parts,)),
            dma((7,)),
            dma((4,)),
            dma((4,)),
            dma((4, 3)),
            dma((4, 3)),
            dma((3, parts - 1)),
            dma((3, parts - 1)),
            dma((parts,)),
            dma((parts,)),
            dma((parts,)),
            dma((parts,)),
            dma((parts - 1,)),
            dma((parts - 1,)),
            dma((GROUP - 1,)),
            dma((GROUP - 1,)),
        ],
        compiler_params=pltpu.CompilerParams(
            collective_id=1, has_side_effects=True, vmem_limit_bytes=64 * 1024 * 1024 - 128 * 1024
        ),
        name="backward_part",
    )(d_ctx, q_t, k_n, v_t, lse, seg_row, seg_col, tokens, g_own, sums, qkv_full, *blocks)


def segment_ids(pair_lengths, count):
    pair_ends = jnp.cumsum(pair_lengths)
    positions = jnp.arange(count, dtype=jnp.int32)
    return jnp.sum((positions[:, None] >= pair_ends[None, :]).astype(jnp.int32), axis=1)


def norm_forward(values, gain, shift_bias):
    average = jnp.mean(values, axis=-1, keepdims=True)
    centred = values - average
    inv_spread = lax.rsqrt(jnp.mean(centred * centred, axis=-1, keepdims=True) + epsilon)
    normed = centred * inv_spread
    return (normed * gain + shift_bias, normed, inv_spread)


def middle_kernel(
    parts, ctx, vecs, b_up, wqkv, x_hbm, g_hbm, out_hbm, up_hbm, down_hbm,
    layer_out, grad_one, d_ctx, sums, g_down, g_up, g_out, w_all,
    out, up, down, act, slope, low, low_t, hid, normed, inv, fed, d_fed, d_fed_t, d_pre,
    v_down, v_up, v_out, x, g, l_sem, s_sem, t_sem, z_send, z_recv, x_send, x_recv, c_send, c_recv, o_sem,
):
    own, model = x.shape
    half = own // 2
    me = lax.axis_index("tensor")
    mine = pl.ds(pl.multiple_of(me * own, own), own)
    rows_in = [pltpu.make_async_copy(a.at[mine, :], b, t_sem.at[i]) for i, (a, b) in enumerate(((x_hbm, x), (g_hbm, g)))]
    for copy in rows_in:
        copy.start()
    loads = [
        pltpu.make_async_copy(a.at[n], b.at[n], l_sem.at[i, n])
        for i, (a, b) in enumerate(((out_hbm, out), (up_hbm, up), (down_hbm, down)))
        for n in range(parts)
    ]
    for load in loads:
        load.start()
    dp = lax.axis_index("dp")
    rank = dp % GROUP
    base = dp - rank
    others = peers_of(rank)

    def at(j):
        return (me + j) % parts

    greet([(dp, at(j)) for j in range(1, parts)] + [(base + other, me) for other in others[:3]])

    def z_copy(j):
        return remote(
            wqkv.at[:, rank], w_all.at[me, :, rank], z_send.at[j - 1], z_recv.at[j - 1], (dp, at(j))
        )

    def x_copy(j, k, slot, to):
        piece = w_all.at[at(parts - j), :, slot]
        return remote(piece, piece, x_send.at[j - 1, k], x_recv.at[j - 1, k], (base + to, me))

    def c_copy(j, k, slot):
        piece = w_all.at[at(parts - j), :, slot]
        return remote(piece, piece, c_send.at[j - 1, k], c_recv.at[j - 1, k], (base + others[0], me))

    for j in range(1, parts):
        z_copy(j).start()
    own_w = pltpu.make_async_copy(wqkv, w_all.at[me], o_sem)
    own_w.start()

    def spread():
        for j in range(1, parts):
            z_copy(j).wait_recv()
            for k in (1, 2):
                x_copy(j, k, rank, others[k]).start()

    def relay():
        for j in range(1, parts):
            x_copy(j, 1, others[1], others[1]).wait_recv()
            x_copy(j, 0, others[1], others[2]).start()
            c_copy(j, 0, rank).start()
            c_copy(j, 1, others[1]).start()

    def pass_on():
        for j in range(1, parts):
            x_copy(j, 2, others[2], others[2]).wait_recv()
            c_copy(j, 2, others[2]).start()
        for j in range(1, parts):
            x_copy(j, 0, others[3], others[2]).wait_recv()
            c_copy(j, 3, others[3]).start()

    b_out, g1, s1, b_down, g2, s2 = [vecs[i : i + 1, :] for i in range(6)]
    sums[...] = jnp.zeros(sums.shape, F32)
    for load in loads[:parts] + rows_in:
        load.wait()

    def rows_of(r):
        return pl.ds(pl.multiple_of(r * half, half), half)

    def add_to(row, values):
        sums[row : row + 1, :] += jnp.sum(values, axis=0, keepdims=True)

    @pl.loop(0, 2)
    def _(r):
        here = rows_of(r)
        mixed = x[here, :].astype(F32) + b_out
        for n in range(parts):
            mixed = mixed + mm(ctx[n, here, :], out[n])
        value, n1, r1 = norm_forward(mixed, g1, s1)
        hid[here, :] = value
        normed[here, :] = n1
        inv[here, :] = jnp.broadcast_to(r1, (half, 128))
        low[here, :] = value.astype(BF16)
        low_t[:, here] = value.T.astype(BF16)
        fed[here, :] = value + b_down

    for load in loads[parts:]:
        load.wait()

    @pl.loop(0, parts * 2)
    def _(t):
        n = t // 2
        here = rows_of(t % 2)
        pre = mm(low[here, :], up[n]) + b_up[pl.ds(n, 1), :]
        share = 0.5 + 0.5 * lax.erf(pre * (0.5**0.5))
        slope[n, here, :] = share + pre * (jnp.exp(-0.5 * pre * pre) * 0.3989422804014327)
        value = (pre * share).astype(BF16)
        act[n, here, :] = value
        fed[here, :] += mm(value, down[n])

        @pl.when(t == 5)
        def _():
            spread()

    @pl.loop(0, 2)
    def _(r):
        here = rows_of(r)
        value, n2, r2 = norm_forward(fed[here, :], g2, s2)
        layer_out[here, :] = value.astype(BF16)
        cot = g[here, :].astype(F32)
        scaled = cot * g2
        grad_two = (
            scaled
            - jnp.mean(scaled, axis=-1, keepdims=True)
            - n2 * jnp.mean(scaled * n2, axis=-1, keepdims=True)
        ) * r2
        add_to(3, grad_two)
        add_to(4, cot * n2)
        add_to(5, cot)
        fed[here, :] = grad_two
        d_fed[here, :] = grad_two.astype(BF16)
        d_fed_t[:, here] = grad_two.T.astype(BF16)

    def store(which, n):
        src, dst = ((v_down, g_down), (v_up, g_up), (v_out, g_out))[which]
        return pltpu.make_async_copy(src.at[n], dst.at[n], s_sem.at[which, n])

    @pl.loop(0, parts)
    def _(n):
        v_down[n] = mm(d_fed_t[...], act[n]).astype(BF16)
        store(0, n).start()

        @pl.loop(0, 2)
        def _(r):
            here = rows_of(r)
            grad = (mm_nt(d_fed[here, :], down[n]) * slope[n, here, :]).astype(BF16)
            d_pre[here, :] = grad
            sums[pl.ds(8 + n, 1), :] += jnp.sum(grad.astype(F32), axis=0, keepdims=True)
            fed[here, :] += mm_nt(grad, up[n])

        v_up[n] = mm(low_t[...], d_pre[...]).astype(BF16)
        store(1, n).start()

        @pl.when(n == 1)
        def _():
            relay()

    @pl.loop(0, 2)
    def _(r):
        here = rows_of(r)
        n1 = normed[here, :]
        grad = fed[here, :]
        scaled = grad * g1
        value = (
            scaled
            - jnp.mean(scaled, axis=-1, keepdims=True)
            - n1 * jnp.mean(scaled * n1, axis=-1, keepdims=True)
        ) * inv[here, 0:1]
        add_to(0, value)
        add_to(1, grad * n1)
        add_to(2, grad)
        grad_one[here, :] = value
        d_fed_t[:, here] = value.T.astype(BF16)
        d_att = value.astype(BF16)
        for n in range(parts):
            d_ctx[n, here, :] = mm_nt(d_att, out[n]).astype(BF16)

    @pl.loop(0, parts)
    def _(n):
        v_out[n] = mm(d_fed_t[...], ctx[n]).astype(BF16)
        store(2, n).start()

    pass_on()
    for which in range(3):
        for n in range(parts):
            store(which, n).wait()
    own_w.wait()
    for j in range(1, parts):
        z_copy(j).wait_send()
        for k in (1, 2):
            x_copy(j, k, rank, others[k]).wait_send()
        x_copy(j, 0, others[3], others[2]).wait_send()
        for k in range(4):
            c_copy(j, k, others[0]).wait()


def middle_part(parts, tokens, cotangent, ctx_all, w_out, w_up, w_down, vecs, b_up, w_qkv):
    own, width = ctx_all.shape[1], ctx_all.shape[2]
    model = w_out.shape[2]
    units = w_up.shape[2]
    vmem = pl.BlockSpec(memory_space=pltpu.VMEM)
    hbm = pl.BlockSpec(memory_space=pl.ANY)
    grads = [(parts, model, units), (parts, model, units), (parts, model, width)]
    pieces = w_qkv.reshape(3, GROUP, width // GROUP, model)
    dma = pltpu.SemaphoreType.DMA
    outs = pl.pallas_call(
        functools.partial(middle_kernel, parts),
        out_shape=[
            jax.ShapeDtypeStruct((own, model), BF16),
            jax.ShapeDtypeStruct((own, model), F32),
            jax.ShapeDtypeStruct(ctx_all.shape, BF16),
            jax.ShapeDtypeStruct((24, model), F32),
        ]
        + [jax.ShapeDtypeStruct(shape, BF16) for shape in grads]
        + [jax.ShapeDtypeStruct((parts,) + pieces.shape, BF16)],
        in_specs=[vmem] * 4 + [hbm] * 5,
        out_specs=[vmem] * 4 + [hbm] * 4,
        scratch_shapes=[
            pltpu.VMEM(w_out.shape, BF16),
            pltpu.VMEM(w_up.shape, BF16),
            pltpu.VMEM(w_down.shape, BF16),
            pltpu.VMEM((parts, own, units), BF16),
            pltpu.VMEM((parts, own, units), F32),
            pltpu.VMEM((own, model), BF16),
            pltpu.VMEM((model, own), BF16),
            pltpu.VMEM((own, model), F32),
            pltpu.VMEM((own, model), F32),
            pltpu.VMEM((own, 128), F32),
            pltpu.VMEM((own, model), F32),
            pltpu.VMEM((own, model), BF16),
            pltpu.VMEM((model, own), BF16),
            pltpu.VMEM((own, units), BF16),
        ]
        + [pltpu.VMEM(shape, BF16) for shape in grads]
        + [pltpu.VMEM((own, model), BF16)] * 2
        + [dma((3, parts))] * 2
        + [dma((2,))]
        + [dma((parts - 1,))] * 2
        + [dma((parts - 1, 3))] * 2
        + [dma((parts - 1, 4))] * 2
        + [dma],
        compiler_params=pltpu.CompilerParams(
            collective_id=2, has_side_effects=True, vmem_limit_bytes=62 * 1024 * 1024
        ),
        name="middle_part",
    )(ctx_all, vecs, b_up, pieces, tokens, cotangent, w_out, w_up, w_down)
    return (*outs[:-1], outs[-1].reshape((parts,) + w_qkv.shape))


def per_device(
    tokens,
    lengths,
    w_qkv,
    b_qv,
    w_out,
    b_out,
    ln1_gain,
    ln1_bias,
    w_up,
    b_up,
    w_down,
    b_down,
    ln2_gain,
    ln2_bias,
    cotangent,
):
    rows = tokens.shape[0]
    width = w_out.shape[0]
    heads = width // HD
    parts = lax.axis_size("tensor")
    share = rows // parts
    me = lax.axis_index("tensor")
    segment = segment_ids(lengths[0], rows)
    seg_row = segment[None, :]
    ends = jnp.broadcast_to(jnp.cumsum(lengths[0])[:, None], (lengths.shape[1], 128))
    w_rows = jnp.transpose(w_qkv, (0, 2, 1))
    bias = b_qv.astype(F32)[:, :, None]
    b_up_rows = jnp.broadcast_to(b_up.astype(F32)[None], (8, b_up.shape[0]))
    q_t, k_n, v_t, lse, seg_col, ctx_all, b_up_full, up_full, down_full, out_full = forward_part(
        parts, tokens, w_rows, bias, seg_row, ends, b_up_rows, w_up, w_down, w_out
    )
    blank = jnp.zeros_like(b_out)
    vecs = jnp.stack([b_out, ln1_gain, ln1_bias, b_down, ln2_gain, ln2_bias, blank, blank]).astype(F32)
    layer_out, grad_one, d_ctx, sums, grad_down, grad_up, grad_out, qkv_full = middle_part(
        parts, tokens, cotangent, ctx_all, out_full, up_full, down_full, vecs, b_up_full, w_rows
    )
    if lax.axis_size("dp") == GROUP:
        grads = [grad_down, grad_up, grad_out]
        d_in, s_down, s_up, s_out, s_qkv, s_sums = backward_part(
            parts, d_ctx, q_t, k_n, v_t, lse, seg_row, seg_col, tokens, qkv_full, grad_one, sums, grads
        )
        deep = sums.shape[1] // GROUP
        own = lax.dynamic_slice_in_dim(s_sums, lax.axis_index("dp") * deep, deep, 1)
        return (
            layer_out,
            d_in,
            s_qkv,
            s_sums[16:18, :width],
            s_out.T,
            own[0],
            own[1],
            own[2],
            s_up,
            lax.dynamic_index_in_dim(s_sums, 8 + me, 0, keepdims=False),
            s_down.T,
            own[3],
            own[4],
            own[5],
        )
    small, up_bias = sums[:6], sums[8 : 8 + parts]
    d_ctx_own = lax.all_to_all(d_ctx, "tensor", 0, 0).reshape(rows, width)
    dq, dk, dv = backward_plain(q_t, k_n, v_t, lse, d_ctx_own, segment)
    d_qkv = jnp.stack([dq, dk, dv])
    grad_qkv_t = jnp.einsum("td,cte->dce", tokens, d_qkv, preferred_element_type=F32)
    qkv_bias = jnp.sum(d_qkv.astype(F32), axis=1)
    partial_input = jnp.einsum("cte,cde->td", d_qkv, w_qkv, preferred_element_type=F32)
    input_share = lax.psum_scatter(
        partial_input.astype(BF16), "tensor", scatter_dimension=0, tiled=True
    ).astype(F32)
    input_grad = (input_share + grad_one).astype(BF16)
    bias_grads = lax.psum(jnp.stack([qkv_bias[0], qkv_bias[2]]), "dp")
    up_bias_grad = lax.psum(lax.psum_scatter(up_bias, "tensor", scatter_dimension=0, tiled=True), "dp")[0]
    small_share = lax.psum_scatter(lax.psum(small, "tensor"), "dp", scatter_dimension=1, tiled=True)
    qkv_share = lax.psum_scatter(grad_qkv_t, "dp", scatter_dimension=0, tiled=True)

    def shared(blocks):
        over = lax.psum_scatter(blocks, "dp", scatter_dimension=1, tiled=True)
        return lax.psum_scatter(over, "tensor", scatter_dimension=0, tiled=True)[0].astype(F32)

    return (
        layer_out,
        input_grad,
        jnp.transpose(qkv_share, (1, 0, 2)),
        bias_grads,
        shared(grad_out).T,
        small_share[0],
        small_share[1],
        small_share[2],
        shared(grad_up),
        up_bias_grad,
        shared(grad_down).T,
        small_share[3],
        small_share[4],
        small_share[5],
    )


def backward_plain(q_t, k_n, v_t, lse, d_ctx, segment):
    width, rows = q_t.shape
    heads = width // HD
    queries = q_t.T.reshape(rows, heads, HD)
    keys = k_n.reshape(rows, heads, HD)
    values = v_t.T.reshape(rows, heads, HD)
    upstream = d_ctx.reshape(rows, heads, HD)
    scale = HD ** (-0.5)
    scores = jnp.einsum("qhd,khd->hqk", queries, keys, preferred_element_type=F32) * scale
    scores = jnp.where((segment[:, None] == segment[None, :])[None], scores, -1e30)
    soft = jnp.exp(scores - lse[..., None])
    dv = jnp.einsum("hqk,qhd->khd", soft.astype(BF16), upstream, preferred_element_type=F32)
    dp = jnp.einsum("qhd,khd->hqk", upstream, values, preferred_element_type=F32)
    ds = (soft * (dp - jnp.sum(dp * soft, axis=-1, keepdims=True))).astype(BF16)
    dq = jnp.einsum("hqk,khd->qhd", ds, keys, preferred_element_type=F32) * scale
    dk = jnp.einsum("hqk,qhd->khd", ds, queries, preferred_element_type=F32) * scale
    return tuple(d.reshape(rows, width).astype(BF16) for d in (dq, dk, dv))


def solution(mesh):
    return jax.shard_map(
        per_device,
        mesh=mesh,
        in_specs=(
            P("dp", None),
            P("dp", None),
            P(None, None, "tensor"),
            P(None, "tensor"),
            P("tensor", None),
            P(),
            P(),
            P(),
            P(None, "tensor"),
            P("tensor"),
            P("tensor", None),
            P(),
            P(),
            P(),
            P("dp", None),
        ),
        out_specs=(
            P(("dp", "tensor"), None),
            P(("dp", "tensor"), None),
            P(None, "dp", "tensor"),
            P(None, "tensor"),
            P("tensor", "dp"),
            P("dp"),
            P("dp"),
            P("dp"),
            P("dp", "tensor"),
            P("tensor"),
            P("tensor", "dp"),
            P("dp"),
            P("dp"),
            P("dp"),
        ),
        check_vma=False,
    )
```

```python
import functools

import jax
import jax.numpy as jnp
from jax import lax
from jax.experimental import pallas as pl
from jax.experimental.pallas import tpu as pltpu
from jax.sharding import PartitionSpec as P

HD = 64
MOST = 512
GROUP = 8
TILE = 256
epsilon = 1e-05
MESH = pl.DeviceIdType.MESH
F32 = jnp.float32
BF16 = jnp.bfloat16


def mm(a, b):
    return lax.dot_general(a, b, (((1,), (0,)), ((), ())), preferred_element_type=F32)


def mm_nt(a, b):
    return lax.dot_general(a, b, (((1,), (1,)), ((), ())), preferred_element_type=F32)


def mm_tn(a, b):
    return lax.dot_general(a, b, (((0,), (0,)), ((), ())), preferred_element_type=F32)


def mm_tt(a, b):
    return lax.dot_general(a, b, (((0,), (1,)), ((), ())), preferred_element_type=F32)


def peers_of(group_rank):
    core = group_rank % 2
    along_x = (group_rank // 2) % 2
    along_y = group_rank // 4
    step_x = 2 - 4 * along_x
    step_y = 4 - 8 * along_y
    return group_rank + 1 - 2 * core, group_rank + step_x, group_rank + step_y, group_rank + step_x + step_y


def greet(devices):
    barrier = pltpu.get_barrier_semaphore()
    for device in devices:
        pl.semaphore_signal(barrier, inc=1, device_id=device, device_id_type=MESH)
    pl.semaphore_wait(barrier, len(devices))


def remote(src, dst, send_sem, recv_sem, device):
    return pltpu.make_async_remote_copy(
        src_ref=src, dst_ref=dst, send_sem=send_sem, recv_sem=recv_sem, device_id=device, device_id_type=MESH
    )


def forward_kernel(
    parts, tok, wqkv, bias, seg_row, ends, b_up, up, down, out,
    q_t, k_n, v_t, lse, seg_col, ctx_all, b_all, up_all, down_all, out_all,
    k_pad, v_pad, ctx, z_send, z_recv, x_send, x_recv, c_send, c_recv, a_send, a_recv, b_send, b_recv, l_sem,
):
    rows = tok.shape[0]
    width = wqkv.shape[1]
    heads = width // HD
    share = rows // parts
    dp = lax.axis_index("dp")
    me = lax.axis_index("tensor")
    rank = dp % GROUP
    base = dp - rank
    others = peers_of(rank)
    shards = (out, up, down)
    fulls = (out_all, up_all, down_all)

    def at(j):
        return (me + j) % parts

    greet([(dp, at(j)) for j in range(1, parts)] + [(base + other, me) for other in others])

    def z_copy(w, j):
        return remote(
            shards[w].at[rank], fulls[w].at[me, rank], z_send.at[w, j - 1], z_recv.at[w, j - 1], (dp, at(j))
        )

    def x_copy(w, j, k, slot, to):
        piece = fulls[w].at[at(parts - j), slot]
        return remote(piece, piece, x_send.at[w, j - 1, k], x_recv.at[w, j - 1, k], (base + to, me))

    through = (1, 1, 2)

    def c_copy(w, j, k, slot):
        source = at(parts - j)
        piece = fulls[w].at[source, slot]
        return remote(piece, piece, c_send.at[w, j - 1, k], c_recv.at[w, j - 1, k], (base + others[0], me))

    def b_copy(j):
        return remote(b_up, b_all.at[me], b_send.at[j - 1], b_recv.at[j - 1], (dp, at(j)))

    for j in range(1, parts):
        b_copy(j).start()
    for w in range(3):
        for j in range(1, parts):
            z_copy(w, j).start()
    b_all[me] = b_up[...]
    own = [pltpu.make_async_copy(shards[w], fulls[w].at[me], l_sem.at[w]) for w in range(3)]
    for copy in own:
        copy.start()

    def spread(w, j):
        z_copy(w, j).wait_recv()
        for k in (1, 2):
            x_copy(w, j, k, rank, others[k]).start()

    def relay(w, j):
        k = through[w]
        x_copy(w, j, k, others[k], others[k]).wait_recv()
        x_copy(w, j, 0, others[k], others[3 - k]).start()
        c_copy(w, j, 0, rank).start()
        c_copy(w, j, k, others[k]).start()

    def pass_on(w, j):
        k = 3 - through[w]
        x_copy(w, j, k, others[k], others[k]).wait_recv()
        c_copy(w, j, k, others[k]).start()
        x_copy(w, j, 0, others[3], others[k]).wait_recv()
        c_copy(w, j, 3, others[3]).start()

    plan = (
        [(0, spread, 1, 1), (1, spread, 1, 2), (2, spread, 1, 3), (4, spread, 2, 1), (5, spread, 2, 2), (6, spread, 2, 3)]
        + [(1, relay, 0, j) for j in range(1, parts)]
        + [(2, relay, 1, 1), (3, relay, 1, 2), (4, relay, 1, 3), (6, relay, 2, 1), (7, relay, 2, 2)]
        + [(5, pass_on, 0, j) for j in range(1, parts)]
        + [(6, pass_on, 1, 1), (7, pass_on, 1, 2)]
    )

    k_pad[:, :MOST] = jnp.zeros((heads, MOST, HD), BF16)
    k_pad[:, MOST + rows :] = jnp.zeros((heads, MOST, HD), BF16)
    v_pad[:, :MOST] = jnp.zeros((width, MOST), BF16)
    v_pad[:, MOST + rows :] = jnp.zeros((width, MOST), BF16)

    @pl.loop(0, rows // TILE)
    def _(t):
        here = pl.ds(pl.multiple_of(t * TILE, TILE), TILE)
        there = pl.ds(pl.multiple_of(t * TILE + MOST, TILE), TILE)
        x = tok[here, :]
        q_t[:, here] = (mm_nt(wqkv[0], x) + bias[0]).astype(BF16)
        keys = mm_nt(x, wqkv[1]).astype(BF16)
        k_n[here, :] = keys
        for h in range(heads):
            k_pad[h, there, :] = keys[:, h * HD : (h + 1) * HD]
        values = (mm_nt(wqkv[2], x) + bias[1]).astype(BF16)
        v_t[:, here] = values
        v_pad[:, there] = values

    for j in range(1, parts):
        spread(0, j)

    @pl.loop(0, (rows + 2 * MOST) // TILE)
    def _(t):
        spot = lax.broadcasted_iota(jnp.int32, (TILE, 128), 0) + (t * TILE - MOST)
        number = jnp.zeros((TILE, 128), jnp.int32)
        for i in range(ends.shape[0]):
            number = number + (spot >= ends[i : i + 1, :]).astype(jnp.int32)
        seg_col[pl.ds(pl.multiple_of(t * TILE, TILE), TILE), :] = jnp.where(spot < 0, -1, number)

    span = TILE + 2 * MOST
    per_block = share // TILE
    scale = HD ** (-0.5)

    def a_copy(j):
        block = at(j)
        return remote(ctx.at[block], ctx_all.at[me], a_send.at[j - 1], a_recv.at[j - 1], (dp, block))

    @pl.loop(0, rows // TILE)
    def _(step):
        block = (me + 1 + step // per_block) % parts
        inner = (step % per_block) * TILE
        begin = block * share + inner
        here = pl.ds(pl.multiple_of(begin, TILE), TILE)
        window = pl.ds(pl.multiple_of(begin, TILE), span)
        allowed_q = seg_row[:, here]
        allowed_k = seg_col[window, :]
        allowed = jnp.concatenate(
            [allowed_k == allowed_q[:, i * 128 : (i + 1) * 128] for i in range(TILE // 128)], axis=1
        )
        outs = []
        for h in range(heads):
            hs = pl.ds(h * HD, HD)
            queries = q_t[hs, here] * jnp.asarray(scale, BF16)
            scores = jnp.where(allowed, mm(k_pad[h, window, :], queries), -1e30)
            top = jnp.max(scores, axis=0, keepdims=True)
            weights = jnp.exp(scores - top)
            total = jnp.sum(weights, axis=0, keepdims=True)
            lse[h : h + 1, here] = top + jnp.log(total)
            outs.append(mm(v_pad[hs, window], weights.astype(BF16)) / total)
        result = jnp.concatenate(outs, axis=0).T.astype(BF16)
        ctx[block, pl.ds(pl.multiple_of(inner, TILE), TILE), :] = result
        for j in range(1, parts):

            @pl.when(step == j * per_block)
            def _(j=j):
                a_copy(j).start()

        for when in range(8):

            @pl.when(step == when)
            def _(when=when):
                for then, what, w, j in plan:
                    if then == when:
                        what(w, j)

    keep = pltpu.make_async_copy(ctx.at[me], ctx_all.at[me], l_sem.at[3])
    keep.start()
    relay(2, 3)
    pass_on(1, 3)
    for j in range(1, parts):
        pass_on(2, j)
    for j in range(1, parts):
        a_copy(j).wait()
        b_copy(j).wait()
    for w in range(3):
        for j in range(1, parts):
            z_copy(w, j).wait_send()
            for k in (1, 2):
                x_copy(w, j, k, rank, others[k]).wait_send()
            x_copy(w, j, 0, others[3], others[3 - through[w]]).wait_send()
            for k in range(4):
                c_copy(w, j, k, others[0]).wait()
    for copy in own:
        copy.wait()
    keep.wait()


def forward_part(parts, tokens, w_qkv, bias, seg_row, ends, b_up, w_up, w_down, w_out):
    rows, model = tokens.shape
    width = w_qkv.shape[1]
    heads = width // HD
    share = rows // parts

    def sliced(w):
        return w.reshape(GROUP, w.shape[0] // GROUP, w.shape[1])

    shards = [sliced(w) for w in (w_up, w_down, w_out)]
    vmem = pl.BlockSpec(memory_space=pltpu.VMEM)
    hbm = pl.BlockSpec(memory_space=pl.ANY)
    dma = pltpu.SemaphoreType.DMA
    outs = pl.pallas_call(
        functools.partial(forward_kernel, parts),
        out_shape=[
            jax.ShapeDtypeStruct((width, rows), BF16),
            jax.ShapeDtypeStruct((rows, width), BF16),
            jax.ShapeDtypeStruct((width, rows), BF16),
            jax.ShapeDtypeStruct((heads, rows), F32),
            jax.ShapeDtypeStruct((rows + 2 * MOST, 128), jnp.int32),
            jax.ShapeDtypeStruct((parts, share, width), BF16),
            jax.ShapeDtypeStruct((parts,) + b_up.shape, F32),
        ]
        + [jax.ShapeDtypeStruct((parts,) + s.shape, BF16) for s in shards],
        in_specs=[vmem] * 9,
        out_specs=[vmem] * 7 + [hbm] * 3,
        scratch_shapes=[
            pltpu.VMEM((heads, rows + 2 * MOST, HD), BF16),
            pltpu.VMEM((width, rows + 2 * MOST), BF16),
            pltpu.VMEM((parts, share, width), BF16),
            dma((3, parts - 1)),
            dma((3, parts - 1)),
            dma((3, parts - 1, 3)),
            dma((3, parts - 1, 3)),
            dma((3, parts - 1, 4)),
            dma((3, parts - 1, 4)),
            dma((parts - 1,)),
            dma((parts - 1,)),
            dma((parts - 1,)),
            dma((parts - 1,)),
            dma((4,)),
        ],
        compiler_params=pltpu.CompilerParams(
            collective_id=0, has_side_effects=True, vmem_limit_bytes=60 * 1024 * 1024
        ),
        name="forward_part",
    )(tokens, w_qkv, bias, seg_row, ends, b_up, *shards)
    q_t, k_n, v_t, lse, seg_col, ctx_all, b_all, up_all, down_all, out_all = outs
    return (
        q_t, k_n, v_t, lse, seg_col, ctx_all, b_all[:, 0],
        up_all.reshape((parts,) + w_up.shape),
        down_all.reshape((parts,) + w_down.shape),
        out_all.reshape((parts,) + w_out.shape),
    )


def backward_kernel(
    parts, d_ctx, q_t, k_n, v_t, lse, seg_row, seg_col, tok, g_own, sums, w_hbm, g_down, g_up, g_out,
    d_in, s_down, s_up, s_out, s_qkv, s_sums,
    dc, k_pad, v_pad, k_t, q_n, acc_k, acc_v, pq, pk, rq, rk, w_all,
    p_down, p_up, p_out, r_down, r_up, r_out, x_down, x_up, x_out, y_down, y_up, y_out, z_down, z_up, z_out,
    gq, r_gq, x_gq, sum_z, sum_dp, sum_in,
    a_send, a_recv, l_sem, s1_send, s1_recv, s2_send, s2_recv, s3_send, s3_recv,
    e_send, e_recv, h_send, h_recv, m_send, m_recv, n_send, n_recv,
):
    rows, model = tok.shape
    width = q_t.shape[0]
    heads = width // HD
    share = rows // parts
    dp = lax.axis_index("dp")
    me = lax.axis_index("tensor")
    rank = dp % GROUP
    base = dp - rank
    core = rank % 2
    chip = rank // 2
    along_y, along_x = chip // 2, chip % 2
    others = peers_of(rank)
    starts = (2, 1, 2)
    full = (g_down, g_up, g_out)
    held = (p_down, p_up, p_out, gq)
    first = (r_down, r_up, r_out, r_gq)
    second = (x_down, x_up, x_out)
    last = (y_down, y_up, y_out)
    third = (z_down, z_up, z_out)
    shared = (s_down, s_up, s_out)
    scale = HD ** (-0.5)

    def at(j):
        return (me + j) % parts

    fellows = [(rank + k) % GROUP for k in range(1, GROUP)]
    greet([(dp, at(j)) for j in range(1, parts)] + [(base + f, me) for f in fellows])

    def order(k):
        return jnp.where(me < parts // 2, (me + k) % parts, (me + parts - k) % parts)

    def a_copy(to):
        return remote(d_ctx.at[to], dc.at[me], a_send.at[to], a_recv.at[me], (dp, to))

    def a_wait(source):
        remote(d_ctx.at[source], dc.at[source], a_send.at[source], a_recv.at[source], (dp, source)).wait_recv()

    def s1_copy(w):
        src = full[w].at[:, :, :, 1 - core] if w < 3 else gq.at[:, 1 - core]
        return remote(src, first[w], s1_send.at[w], s1_recv.at[w], (base + others[0], me))

    def s2_copy(w):
        if starts[w] == 1:
            src = held[w].at[:, :, 1 - along_x]
        else:
            src = held[w].at[:, 1 - along_y]
        return remote(src, second[w], s2_send.at[w, 0], s2_recv.at[w, 0], (base + others[starts[w]], me))

    def s2_then(w):
        if starts[w] == 1:
            src = held[w].at[:, 1 - along_y, along_x]
        else:
            src = held[w].at[:, along_y, 1 - along_x]
        return remote(src, last[w], s2_send.at[w, 1], s2_recv.at[w, 1], (base + others[3 - starts[w]], me))

    def gq_copy(k):
        to = others[1 + k]
        return remote(gq.at[to // 2, core], x_gq.at[k], s2_send.at[3, k], s2_recv.at[3, k], (base + to, me))

    def s3_copy(w, j):
        return remote(
            held[w].at[at(j), along_y, along_x],
            third[w].at[j - 1],
            s3_send.at[w, j - 1],
            s3_recv.at[w, j - 1],
            (dp, at(j)),
        )

    def m_copy(j):
        return remote(sums, sum_z.at[j - 1], m_send.at[j - 1], m_recv.at[j - 1], (dp, at(j)))

    def n_copy(k):
        return remote(sum_in, sum_dp.at[k], n_send.at[k], n_recv.at[k], (base + fellows[k], me))

    for k in range(1, parts):
        a_copy(order(k)).start()
    for j in range(1, parts):
        m_copy(j).start()
    loads = [pltpu.make_async_copy(full[w].at[:, :, :, core], held[w], l_sem.at[w]) for w in range(3)]
    for w in range(3):
        s1_copy(w).start()
        loads[w].start()
    mine = pltpu.make_async_copy(d_ctx.at[me], dc.at[me], l_sem.at[3])
    mine.start()
    whole = pltpu.make_async_copy(w_hbm, w_all, l_sem.at[4])
    whole.start()

    for ref in (k_pad, v_pad):
        ref[:MOST, :] = jnp.zeros((MOST, width), BF16)
        ref[MOST + rows :, :] = jnp.zeros((MOST, width), BF16)
    k_t[:, :MOST] = jnp.zeros((width, MOST), BF16)
    k_t[:, MOST + rows :] = jnp.zeros((width, MOST), BF16)

    @pl.loop(0, rows // TILE)
    def _(t):
        here = pl.ds(pl.multiple_of(t * TILE, TILE), TILE)
        there = pl.ds(pl.multiple_of(t * TILE + MOST, TILE), TILE)
        keys = k_n[here, :]
        k_pad[there, :] = keys
        k_t[:, there] = keys.astype(F32).T.astype(BF16)
        v_pad[there, :] = v_t[:, here].astype(F32).T.astype(BF16)
        q_n[here, :] = (q_t[:, here].astype(F32) * scale).T.astype(BF16)

    @pl.loop(0, (rows + 2 * MOST) // TILE)
    def _(t):
        here = pl.ds(pl.multiple_of(t * TILE, TILE), TILE)
        acc_k[here, :] = jnp.zeros((TILE, width), F32)
        acc_v[here, :] = jnp.zeros((TILE, width), F32)

    def s1_finish(w):
        s1_copy(w).wait_recv()
        loads[w].wait()

        @pl.loop(0, parts)
        def _(n):
            for c in range(GROUP // 2):
                at_c = (n, c // 2, c % 2)
                held[w][at_c] = (held[w][at_c].astype(F32) + first[w][at_c].astype(F32)).astype(BF16)

        s2_copy(w).start()

    def s2_finish(w):
        s2_copy(w).wait_recv()

        @pl.loop(0, parts)
        def _(n):
            for c in range(2):
                at_c = (n, c, along_x) if starts[w] == 1 else (n, along_y, c)
                held[w][at_c] = (held[w][at_c].astype(F32) + second[w][n, c].astype(F32)).astype(BF16)

        s2_then(w).start()

    def s2_end(w):
        s2_then(w).wait_recv()

        @pl.loop(0, parts)
        def _(n):
            here = (n, along_y, along_x)
            held[w][here] = (held[w][here].astype(F32) + last[w][n].astype(F32)).astype(BF16)

        for j in range(1, parts):
            s3_copy(w, j).start()

    def s3_finish(w):
        for j in range(1, parts):
            s3_copy(w, j).wait_recv()
        total = held[w][me, along_y, along_x].astype(F32)
        for j in range(1, parts):
            total = total + third[w][j - 1].astype(F32)
        shared[w][...] = total

    span = TILE + 2 * MOST
    per_block = share // TILE
    mine.wait()

    def tile(block, inner):
        begin = block * share + inner
        here = pl.ds(pl.multiple_of(begin, TILE), TILE)
        window = pl.ds(pl.multiple_of(begin, TILE), span)
        allowed_q = seg_row[:, here]
        allowed_k = seg_col[window, :]
        allowed = jnp.concatenate(
            [allowed_k == allowed_q[:, i * 128 : (i + 1) * 128] for i in range(TILE // 128)], axis=1
        )
        up_n = dc[block, pl.ds(pl.multiple_of(inner, TILE), TILE), :]
        up_t = up_n.astype(F32).T.astype(BF16)
        grads_k = []
        grads_v = []
        for h in range(heads):
            hs = slice(h * HD, (h + 1) * HD)
            queries = q_t[hs, here] * jnp.asarray(scale, BF16)
            scores = jnp.where(allowed, mm(k_pad[window, :][:, hs], queries), -1e30)
            soft = jnp.exp(scores - lse[h : h + 1, here])
            grad = mm(v_pad[window, :][:, hs], up_t[hs, :])
            shift = jnp.sum(grad * soft, axis=0, keepdims=True)
            inner_grad = (soft * (grad - shift)).astype(BF16)
            grads_v.append(mm(soft.astype(BF16), up_n[:, hs]))
            grads_k.append(mm(inner_grad, q_n[here, :][:, hs]))
            grad_q = (mm(k_t[hs, window], inner_grad) * scale).astype(BF16)
            pq[block, hs, pl.ds(pl.multiple_of(inner, TILE), TILE)] = grad_q
        acc_k[window, :] += jnp.concatenate(grads_k, axis=1)
        acc_v[window, :] += jnp.concatenate(grads_v, axis=1)

    def q_copy(b):
        return remote(pq.at[b], rq.at[me], e_send.at[b], e_recv.at[me], (dp, b))

    def k_copy(b):
        return remote(pk.at[b], rk.at[me], h_send.at[b], h_recv.at[me], (dp, b))

    def e_wait(m):
        remote(pq.at[m], rq.at[m], e_send.at[m], e_recv.at[m], (dp, m)).wait_recv()
        remote(pk.at[m], rk.at[m], h_send.at[m], h_recv.at[m], (dp, m)).wait_recv()

    def finish(b):
        @pl.loop(0, per_block)
        def _(t):
            there = pl.ds(pl.multiple_of(b * share + t * TILE + MOST, TILE), TILE)
            pair = jnp.concatenate([acc_k[there, :], acc_v[there, :]], axis=1)
            pk[b, pl.ds(pl.multiple_of(t * TILE, TILE), TILE), :] = pair.astype(BF16)

        @pl.when(b != me)
        def _():
            q_copy(b).start()
            k_copy(b).start()

    final = order(parts - 1)
    @pl.loop(0, parts)
    def _(k):
        block = order(k)

        @pl.when(k > 0)
        def _():
            a_wait(block)

        @pl.loop(0, per_block)
        def _(t):
            tile(block, t * TILE)

        for when, what, w in ((0, s1_finish, 0), (0, s1_finish, 1), (1, s1_finish, 2)):

            @pl.when(k == when)
            def _(what=what, w=w):
                what(w)

        @pl.when(k >= parts - 2)
        def _():
            @pl.loop(0, parts)
            def _(b):
                early = (b - final >= 2) | (final - b >= 2)

                @pl.when(early == (k == parts - 2))
                def _():
                    finish(b)

    keep_q = pltpu.make_async_copy(pq.at[me], rq.at[me], l_sem.at[5])
    keep_k = pltpu.make_async_copy(pk.at[me], rk.at[me], l_sem.at[6])
    keep_q.start()
    keep_k.start()
    s2_finish(0)
    s2_finish(1)

    deep = model // GROUP
    rows_b = [slice(b * share, (b + 1) * share) for b in range(parts)]
    grads_q = sum(mm(pq[b], tok[rows_b[b], :]) for b in range(parts))
    grads_kv = sum(mm_tn(pk[b], tok[rows_b[b], :]) for b in range(parts))
    for c, grads in enumerate((grads_q, grads_kv[:width], grads_kv[width:])):
        grads = grads.T.astype(BF16)
        for i in range(GROUP):
            gq[i // 2, i % 2, c] = grads[i * deep : (i + 1) * deep, :]
    s1_copy(3).start()
    for j in range(1, parts):
        m_copy(j).wait_recv()
    total = sums[...]
    for j in range(1, parts):
        total = total + sum_z[j - 1]
    sum_in[...] = total
    keep = sum_in.shape[0] - 8
    flat_q = sum(jnp.sum(pq[b].astype(F32), axis=1, keepdims=True) for b in range(parts)).T
    flat_v = sum(jnp.sum(pk[b].astype(F32), axis=0, keepdims=True) for b in range(parts))[:, width:]
    sum_in[keep : keep + 1, :width] = flat_q
    sum_in[keep + 1 : keep + 2, :width] = flat_v
    for k in range(GROUP - 1):
        n_copy(k).start()

    s1_copy(3).wait_recv()
    for c in range(GROUP // 2):
        for i in range(3):
            gq[c, core, i] = (gq[c, core, i].astype(F32) + r_gq[c, i].astype(F32)).astype(BF16)
    s2_finish(2)
    for k in range(3):
        gq_copy(k).start()
    s2_end(0)
    s2_end(1)
    s2_end(2)
    whole.wait()
    keep_q.wait()
    keep_k.wait()
    for j in range(1, parts):
        e_wait(at(j))

    @pl.loop(0, per_block)
    def _(t):
        here = pl.ds(pl.multiple_of(t * TILE, TILE), TILE)
        total = g_own[here, :]
        for m in range(parts):
            pair = rk[m, here, :]
            total = total + mm_tn(rq[m, :, here], w_all[m, 0])
            total = total + mm(pair[:, :width], w_all[m, 1]) + mm(pair[:, width:], w_all[m, 2])
        d_in[here, :] = total.astype(BF16)

    for k in range(3):
        gq_copy(k).wait_recv()
    for i in range(3):
        block = gq[chip, core, i].astype(F32)
        for k in range(3):
            block = block + x_gq[k, i].astype(F32)
        s_qkv[i] = block
    for k in range(GROUP - 1):
        n_copy(k).wait()
    total = sum_in[...]
    for k in range(GROUP - 1):
        total = total + sum_dp[k]
    s_sums[...] = total
    for w in range(3):
        s3_finish(w)

    for k in range(1, parts):
        a_copy(order(k)).wait_send()
        q_copy(order(k)).wait_send()
        k_copy(order(k)).wait_send()

    for j in range(1, parts):
        m_copy(j).wait_send()
    for w in range(4):
        s1_copy(w).wait_send()
    for w in range(3):
        gq_copy(w).wait_send()
        s2_copy(w).wait_send()
        s2_then(w).wait_send()
    for w in range(3):
        for j in range(1, parts):
            s3_copy(w, j).wait_send()


def backward_part(parts, d_ctx, q_t, k_n, v_t, lse, seg_row, seg_col, tokens, qkv_full, g_own, sums, grads):
    rows, model = tokens.shape
    width = q_t.shape[0]
    heads = width // HD
    share = rows // parts
    deep = model // GROUP
    wides = [g.shape[2] for g in grads]
    blocks = [g.reshape(parts, 2, 2, 2, deep, g.shape[2]) for g in grads]
    vmem = pl.BlockSpec(memory_space=pltpu.VMEM)
    hbm = pl.BlockSpec(memory_space=pl.ANY)
    dma = pltpu.SemaphoreType.DMA
    padded = rows + 2 * MOST

    def held(*lead):
        return [pltpu.VMEM(lead + (deep, w), BF16) for w in wides]

    return pl.pallas_call(
        functools.partial(backward_kernel, parts),
        out_shape=[jax.ShapeDtypeStruct((share, model), BF16)]
        + [jax.ShapeDtypeStruct((deep, w), F32) for w in wides]
        + [jax.ShapeDtypeStruct((3, deep, width), F32), jax.ShapeDtypeStruct(sums.shape, F32)],
        in_specs=[vmem] * 10 + [hbm] * 4,
        out_specs=[vmem] * 6,
        scratch_shapes=[
            pltpu.VMEM((parts, share, width), BF16),
            pltpu.VMEM((padded, width), BF16),
            pltpu.VMEM((padded, width), BF16),
            pltpu.VMEM((width, padded), BF16),
            pltpu.VMEM((rows, width), BF16),
            pltpu.VMEM((padded, width), F32),
            pltpu.VMEM((padded, width), F32),
            pltpu.VMEM((parts, width, share), BF16),
            pltpu.VMEM((parts, share, 2 * width), BF16),
            pltpu.VMEM((parts, width, share), BF16),
            pltpu.VMEM((parts, share, 2 * width), BF16),
            pltpu.VMEM(qkv_full.shape, BF16),
        ]
        + held(parts, 2, 2)
        + held(parts, 2, 2)
        + held(parts, 2)
        + held(parts)
        + held(parts - 1)
        + [
            pltpu.VMEM((GROUP // 2, 2, 3, deep, width), BF16),
            pltpu.VMEM((GROUP // 2, 3, deep, width), BF16),
            pltpu.VMEM((3, 3, deep, width), BF16),
            pltpu.VMEM((parts - 1,) + sums.shape, F32),
            pltpu.VMEM((GROUP - 1,) + sums.shape, F32),
            pltpu.VMEM(sums.shape, F32),
            dma((parts,)),
            dma((parts,)),
            dma((7,)),
            dma((4,)),
            dma((4,)),
            dma((4, 3)),
            dma((4, 3)),
            dma((3, parts - 1)),
            dma((3, parts - 1)),
            dma((parts,)),
            dma((parts,)),
            dma((parts,)),
            dma((parts,)),
            dma((parts - 1,)),
            dma((parts - 1,)),
            dma((GROUP - 1,)),
            dma((GROUP - 1,)),
        ],
        compiler_params=pltpu.CompilerParams(
            collective_id=1, has_side_effects=True, vmem_limit_bytes=64 * 1024 * 1024 - 128 * 1024
        ),
        name="backward_part",
    )(d_ctx, q_t, k_n, v_t, lse, seg_row, seg_col, tokens, g_own, sums, qkv_full, *blocks)


def segment_ids(pair_lengths, count):
    pair_ends = jnp.cumsum(pair_lengths)
    positions = jnp.arange(count, dtype=jnp.int32)
    return jnp.sum((positions[:, None] >= pair_ends[None, :]).astype(jnp.int32), axis=1)


def norm_forward(values, gain, shift_bias):
    average = jnp.mean(values, axis=-1, keepdims=True)
    centred = values - average
    inv_spread = lax.rsqrt(jnp.mean(centred * centred, axis=-1, keepdims=True) + epsilon)
    normed = centred * inv_spread
    return (normed * gain + shift_bias, normed, inv_spread)


def middle_kernel(
    parts, ctx, vecs, b_up, wqkv, x_hbm, g_hbm, out_hbm, up_hbm, down_hbm,
    layer_out, grad_one, d_ctx, sums, g_down, g_up, g_out, w_all,
    out, up, down, act, slope, low, low_t, hid, normed, inv, fed, d_fed, d_fed_t, d_pre,
    v_down, v_up, v_out, x, g, l_sem, s_sem, t_sem, z_send, z_recv, x_send, x_recv, c_send, c_recv, o_sem,
):
    own, model = x.shape
    half = own // 2
    me = lax.axis_index("tensor")
    mine = pl.ds(pl.multiple_of(me * own, own), own)
    rows_in = [pltpu.make_async_copy(a.at[mine, :], b, t_sem.at[i]) for i, (a, b) in enumerate(((x_hbm, x), (g_hbm, g)))]
    for copy in rows_in:
        copy.start()
    loads = [
        pltpu.make_async_copy(a.at[n], b.at[n], l_sem.at[i, n])
        for i, (a, b) in enumerate(((out_hbm, out), (up_hbm, up), (down_hbm, down)))
        for n in range(parts)
    ]
    for load in loads:
        load.start()
    dp = lax.axis_index("dp")
    rank = dp % GROUP
    base = dp - rank
    others = peers_of(rank)

    def at(j):
        return (me + j) % parts

    greet([(dp, at(j)) for j in range(1, parts)] + [(base + other, me) for other in others[:3]])

    def z_copy(j):
        return remote(
            wqkv.at[:, rank], w_all.at[me, :, rank], z_send.at[j - 1], z_recv.at[j - 1], (dp, at(j))
        )

    def x_copy(j, k, slot, to):
        piece = w_all.at[at(parts - j), :, slot]
        return remote(piece, piece, x_send.at[j - 1, k], x_recv.at[j - 1, k], (base + to, me))

    def c_copy(j, k, slot):
        piece = w_all.at[at(parts - j), :, slot]
        return remote(piece, piece, c_send.at[j - 1, k], c_recv.at[j - 1, k], (base + others[0], me))

    for j in range(1, parts):
        z_copy(j).start()
    own_w = pltpu.make_async_copy(wqkv, w_all.at[me], o_sem)
    own_w.start()

    def spread():
        for j in range(1, parts):
            z_copy(j).wait_recv()
            for k in (1, 2):
                x_copy(j, k, rank, others[k]).start()

    def relay():
        for j in range(1, parts):
            x_copy(j, 1, others[1], others[1]).wait_recv()
            x_copy(j, 0, others[1], others[2]).start()
            c_copy(j, 0, rank).start()
            c_copy(j, 1, others[1]).start()

    def pass_on():
        for j in range(1, parts):
            x_copy(j, 2, others[2], others[2]).wait_recv()
            c_copy(j, 2, others[2]).start()
        for j in range(1, parts):
            x_copy(j, 0, others[3], others[2]).wait_recv()
            c_copy(j, 3, others[3]).start()

    b_out, g1, s1, b_down, g2, s2 = [vecs[i : i + 1, :] for i in range(6)]
    sums[...] = jnp.zeros(sums.shape, F32)
    for load in loads[:parts] + rows_in:
        load.wait()

    def rows_of(r):
        return pl.ds(pl.multiple_of(r * half, half), half)

    def add_to(row, values):
        sums[row : row + 1, :] += jnp.sum(values, axis=0, keepdims=True)

    @pl.loop(0, 2)
    def _(r):
        here = rows_of(r)
        mixed = x[here, :].astype(F32) + b_out
        for n in range(parts):
            mixed = mixed + mm(ctx[n, here, :], out[n])
        value, n1, r1 = norm_forward(mixed, g1, s1)
        hid[here, :] = value
        normed[here, :] = n1
        inv[here, :] = jnp.broadcast_to(r1, (half, 128))
        low[here, :] = value.astype(BF16)
        low_t[:, here] = value.T.astype(BF16)
        fed[here, :] = value + b_down

    for load in loads[parts:]:
        load.wait()

    @pl.loop(0, parts * 2)
    def _(t):
        n = t // 2
        here = rows_of(t % 2)
        pre = mm(low[here, :], up[n]) + b_up[pl.ds(n, 1), :]
        share = 0.5 + 0.5 * lax.erf(pre * (0.5**0.5))
        slope[n, here, :] = share + pre * (jnp.exp(-0.5 * pre * pre) * 0.3989422804014327)
        value = (pre * share).astype(BF16)
        act[n, here, :] = value
        fed[here, :] += mm(value, down[n])

        @pl.when(t == 5)
        def _():
            spread()

    @pl.loop(0, 2)
    def _(r):
        here = rows_of(r)
        value, n2, r2 = norm_forward(fed[here, :], g2, s2)
        layer_out[here, :] = value.astype(BF16)
        cot = g[here, :].astype(F32)
        scaled = cot * g2
        grad_two = (
            scaled
            - jnp.mean(scaled, axis=-1, keepdims=True)
            - n2 * jnp.mean(scaled * n2, axis=-1, keepdims=True)
        ) * r2
        add_to(3, grad_two)
        add_to(4, cot * n2)
        add_to(5, cot)
        fed[here, :] = grad_two
        d_fed[here, :] = grad_two.astype(BF16)
        d_fed_t[:, here] = grad_two.T.astype(BF16)

    def store(which, n):
        src, dst = ((v_down, g_down), (v_up, g_up), (v_out, g_out))[which]
        return pltpu.make_async_copy(src.at[n], dst.at[n], s_sem.at[which, n])

    @pl.loop(0, parts)
    def _(n):
        v_down[n] = mm(d_fed_t[...], act[n]).astype(BF16)
        store(0, n).start()

        @pl.loop(0, 2)
        def _(r):
            here = rows_of(r)
            grad = (mm_nt(d_fed[here, :], down[n]) * slope[n, here, :]).astype(BF16)
            d_pre[here, :] = grad
            sums[pl.ds(8 + n, 1), :] += jnp.sum(grad.astype(F32), axis=0, keepdims=True)
            fed[here, :] += mm_nt(grad, up[n])

        v_up[n] = mm(low_t[...], d_pre[...]).astype(BF16)
        store(1, n).start()

        @pl.when(n == 1)
        def _():
            relay()

    @pl.loop(0, 2)
    def _(r):
        here = rows_of(r)
        n1 = normed[here, :]
        grad = fed[here, :]
        scaled = grad * g1
        value = (
            scaled
            - jnp.mean(scaled, axis=-1, keepdims=True)
            - n1 * jnp.mean(scaled * n1, axis=-1, keepdims=True)
        ) * inv[here, 0:1]
        add_to(0, value)
        add_to(1, grad * n1)
        add_to(2, grad)
        grad_one[here, :] = value
        d_fed_t[:, here] = value.T.astype(BF16)
        d_att = value.astype(BF16)
        for n in range(parts):
            d_ctx[n, here, :] = mm_nt(d_att, out[n]).astype(BF16)

    @pl.loop(0, parts)
    def _(n):
        v_out[n] = mm(d_fed_t[...], ctx[n]).astype(BF16)
        store(2, n).start()

    pass_on()
    for which in range(3):
        for n in range(parts):
            store(which, n).wait()
    own_w.wait()
    for j in range(1, parts):
        z_copy(j).wait_send()
        for k in (1, 2):
            x_copy(j, k, rank, others[k]).wait_send()
        x_copy(j, 0, others[3], others[2]).wait_send()
        for k in range(4):
            c_copy(j, k, others[0]).wait()


def middle_part(parts, tokens, cotangent, ctx_all, w_out, w_up, w_down, vecs, b_up, w_qkv):
    own, width = ctx_all.shape[1], ctx_all.shape[2]
    model = w_out.shape[2]
    units = w_up.shape[2]
    vmem = pl.BlockSpec(memory_space=pltpu.VMEM)
    hbm = pl.BlockSpec(memory_space=pl.ANY)
    grads = [(parts, model, units), (parts, model, units), (parts, model, width)]
    pieces = w_qkv.reshape(3, GROUP, width // GROUP, model)
    dma = pltpu.SemaphoreType.DMA
    outs = pl.pallas_call(
        functools.partial(middle_kernel, parts),
        out_shape=[
            jax.ShapeDtypeStruct((own, model), BF16),
            jax.ShapeDtypeStruct((own, model), F32),
            jax.ShapeDtypeStruct(ctx_all.shape, BF16),
            jax.ShapeDtypeStruct((24, model), F32),
        ]
        + [jax.ShapeDtypeStruct(shape, BF16) for shape in grads]
        + [jax.ShapeDtypeStruct((parts,) + pieces.shape, BF16)],
        in_specs=[vmem] * 4 + [hbm] * 5,
        out_specs=[vmem] * 4 + [hbm] * 4,
        scratch_shapes=[
            pltpu.VMEM(w_out.shape, BF16),
            pltpu.VMEM(w_up.shape, BF16),
            pltpu.VMEM(w_down.shape, BF16),
            pltpu.VMEM((parts, own, units), BF16),
            pltpu.VMEM((parts, own, units), F32),
            pltpu.VMEM((own, model), BF16),
            pltpu.VMEM((model, own), BF16),
            pltpu.VMEM((own, model), F32),
            pltpu.VMEM((own, model), F32),
            pltpu.VMEM((own, 128), F32),
            pltpu.VMEM((own, model), F32),
            pltpu.VMEM((own, model), BF16),
            pltpu.VMEM((model, own), BF16),
            pltpu.VMEM((own, units), BF16),
        ]
        + [pltpu.VMEM(shape, BF16) for shape in grads]
        + [pltpu.VMEM((own, model), BF16)] * 2
        + [dma((3, parts))] * 2
        + [dma((2,))]
        + [dma((parts - 1,))] * 2
        + [dma((parts - 1, 3))] * 2
        + [dma((parts - 1, 4))] * 2
        + [dma],
        compiler_params=pltpu.CompilerParams(
            collective_id=2, has_side_effects=True, vmem_limit_bytes=62 * 1024 * 1024
        ),
        name="middle_part",
    )(ctx_all, vecs, b_up, pieces, tokens, cotangent, w_out, w_up, w_down)
    return (*outs[:-1], outs[-1].reshape((parts,) + w_qkv.shape))


def per_device(
    tokens,
    lengths,
    w_qkv,
    b_qv,
    w_out,
    b_out,
    ln1_gain,
    ln1_bias,
    w_up,
    b_up,
    w_down,
    b_down,
    ln2_gain,
    ln2_bias,
    cotangent,
):
    rows = tokens.shape[0]
    width = w_out.shape[0]
    heads = width // HD
    parts = lax.axis_size("tensor")
    share = rows // parts
    me = lax.axis_index("tensor")
    segment = segment_ids(lengths[0], rows)
    seg_row = segment[None, :]
    ends = jnp.broadcast_to(jnp.cumsum(lengths[0])[:, None], (lengths.shape[1], 128))
    w_rows = jnp.transpose(w_qkv, (0, 2, 1))
    bias = b_qv.astype(F32)[:, :, None]
    b_up_rows = jnp.broadcast_to(b_up.astype(F32)[None], (8, b_up.shape[0]))
    q_t, k_n, v_t, lse, seg_col, ctx_all, b_up_full, up_full, down_full, out_full = forward_part(
        parts, tokens, w_rows, bias, seg_row, ends, b_up_rows, w_up, w_down, w_out
    )
    blank = jnp.zeros_like(b_out)
    vecs = jnp.stack([b_out, ln1_gain, ln1_bias, b_down, ln2_gain, ln2_bias, blank, blank]).astype(F32)
    layer_out, grad_one, d_ctx, sums, grad_down, grad_up, grad_out, qkv_full = middle_part(
        parts, tokens, cotangent, ctx_all, out_full, up_full, down_full, vecs, b_up_full, w_rows
    )
    if lax.axis_size("dp") == GROUP:
        grads = [grad_down, grad_up, grad_out]
        d_in, s_down, s_up, s_out, s_qkv, s_sums = backward_part(
            parts, d_ctx, q_t, k_n, v_t, lse, seg_row, seg_col, tokens, qkv_full, grad_one, sums, grads
        )
        deep = sums.shape[1] // GROUP
        own = lax.dynamic_slice_in_dim(s_sums, lax.axis_index("dp") * deep, deep, 1)
        return (
            layer_out,
            d_in,
            s_qkv,
            s_sums[16:18, :width],
            s_out.T,
            own[0],
            own[1],
            own[2],
            s_up,
            lax.dynamic_index_in_dim(s_sums, 8 + me, 0, keepdims=False),
            s_down.T,
            own[3],
            own[4],
            own[5],
        )
    small, up_bias = sums[:6], sums[8 : 8 + parts]
    d_ctx_own = lax.all_to_all(d_ctx, "tensor", 0, 0).reshape(rows, width)
    dq, dk, dv = backward_plain(q_t, k_n, v_t, lse, d_ctx_own, segment)
    d_qkv = jnp.stack([dq, dk, dv])
    grad_qkv_t = jnp.einsum("td,cte->dce", tokens, d_qkv, preferred_element_type=F32)
    qkv_bias = jnp.sum(d_qkv.astype(F32), axis=1)
    partial_input = jnp.einsum("cte,cde->td", d_qkv, w_qkv, preferred_element_type=F32)
    input_share = lax.psum_scatter(
        partial_input.astype(BF16), "tensor", scatter_dimension=0, tiled=True
    ).astype(F32)
    input_grad = (input_share + grad_one).astype(BF16)
    bias_grads = lax.psum(jnp.stack([qkv_bias[0], qkv_bias[2]]), "dp")
    up_bias_grad = lax.psum(lax.psum_scatter(up_bias, "tensor", scatter_dimension=0, tiled=True), "dp")[0]
    small_share = lax.psum_scatter(lax.psum(small, "tensor"), "dp", scatter_dimension=1, tiled=True)
    qkv_share = lax.psum_scatter(grad_qkv_t, "dp", scatter_dimension=0, tiled=True)

    def shared(blocks):
        over = lax.psum_scatter(blocks, "dp", scatter_dimension=1, tiled=True)
        return lax.psum_scatter(over, "tensor", scatter_dimension=0, tiled=True)[0].astype(F32)

    return (
        layer_out,
        input_grad,
        jnp.transpose(qkv_share, (1, 0, 2)),
        bias_grads,
        shared(grad_out).T,
        small_share[0],
        small_share[1],
        small_share[2],
        shared(grad_up),
        up_bias_grad,
        shared(grad_down).T,
        small_share[3],
        small_share[4],
        small_share[5],
    )


def backward_plain(q_t, k_n, v_t, lse, d_ctx, segment):
    width, rows = q_t.shape
    heads = width // HD
    queries = q_t.T.reshape(rows, heads, HD)
    keys = k_n.reshape(rows, heads, HD)
    values = v_t.T.reshape(rows, heads, HD)
    upstream = d_ctx.reshape(rows, heads, HD)
    scale = HD ** (-0.5)
    scores = jnp.einsum("qhd,khd->hqk", queries, keys, preferred_element_type=F32) * scale
    scores = jnp.where((segment[:, None] == segment[None, :])[None], scores, -1e30)
    soft = jnp.exp(scores - lse[..., None])
    dv = jnp.einsum("hqk,qhd->khd", soft.astype(BF16), upstream, preferred_element_type=F32)
    dp = jnp.einsum("qhd,khd->hqk", upstream, values, preferred_element_type=F32)
    ds = (soft * (dp - jnp.sum(dp * soft, axis=-1, keepdims=True))).astype(BF16)
    dq = jnp.einsum("hqk,khd->qhd", ds, keys, preferred_element_type=F32) * scale
    dk = jnp.einsum("hqk,qhd->khd", ds, queries, preferred_element_type=F32) * scale
    return tuple(d.reshape(rows, width).astype(BF16) for d in (dq, dk, dv))


def solution(mesh):
    return jax.shard_map(
        per_device,
        mesh=mesh,
        in_specs=(
            P("dp", None),
            P("dp", None),
            P(None, None, "tensor"),
            P(None, "tensor"),
            P("tensor", None),
            P(),
            P(),
            P(),
            P(None, "tensor"),
            P("tensor"),
            P("tensor", None),
            P(),
            P(),
            P(),
            P("dp", None),
        ),
        out_specs=(
            P(("dp", "tensor"), None),
            P(("dp", "tensor"), None),
            P(None, "dp", "tensor"),
            P(None, "tensor"),
            P("tensor", "dp"),
            P("dp"),
            P("dp"),
            P("dp"),
            P("dp", "tensor"),
            P("tensor"),
            P("tensor", "dp"),
            P("dp"),
            P("dp"),
            P("dp"),
        ),
        check_vma=False,
    )
```
